32 devices in a mesh: groups: 2 (over y), orient: 4 (over z), cls: 2 (over x), dom: 2 (over core).
Axes of the slice: x: 2, y: 2, z: 4, core: 2. Of those that a mesh axis runs over, the one named last changes fastest.
Arguments:
- particles: bfloat16 [256, 2, 16512], P(('groups', 'orient', 'cls', 'dom')), parts along dimension 0, may hold values from -10 to 10
- ctf_index: int32 [256], P(('groups', 'orient', 'cls', 'dom')), parts along dimension 0, may hold values from 0 to 15
- beta: bfloat16 [256], P(('groups', 'orient', 'cls', 'dom')), parts along dimension 0, may hold values from 10 to 60
- significant: int32 [128, 1], P(('groups', 'orient', 'cls', 'dom')), parts along dimension 0, may hold values from 0 to 3; in each aligned block of 4 rows (0 to 3, 4 to 7, ...) at most 2 rows name the same one
- ctf_table: bfloat16 [16, 16512], replicated, may hold values from 0.049804688 to 1
- references: bfloat16 [4, 4, 4, 2, 16512], P(('groups', 'cls'), 'orient'), parts along dimension 0, may hold values from -4 to 4
- offsets: int32 [10, 2], P('groups'), parts along dimension 0, may hold values from -3 to 3, as said below
Outputs:
- class_post: float32 [256, 2], P(('groups', 'orient', 'cls', 'dom')), parts along dimension 0
- log_evidence: float32 [256], P(('groups', 'orient', 'cls', 'dom')), parts along dimension 0
The draws below stay inside these ranges and needn't reach their ends.
There are 2 independent parts, one for each index of `groups`. The reference program is written for one: setup_inputs(seed, part) draws one part's arguments, and reference() takes and returns one part's arrays. A program takes and returns all parts, laid end to end along the dimension named above; an argument that names none is the same for every part. Nothing has to cross between parts.
Inputs may be any that keep to these rules, and one draw needn't show every extreme that they name: `significant`: each block of 2 particles names 1 different orientation groups; the 4 blocks of one device name any one group at most 2 times. The 5 offsets are distinct pairs.
All inputs are finite; a program needn't handle non-finite values.
Results may differ from the reference program's by a relative error of at most 0.0003.
Values may be sent and summed in bfloat16 or wider, within the bound.
No kernel may reach another device: no remote copies, remote signals or barrier semaphores. Data moves between devices by JAX's collectives and lax.ppermute only.
A program may use at most 128 MiB of HBM per device.

```python
import math
import jax
import jax.numpy as jnp
import numpy as np
from jax import lax

BOX = 256
KX = 129
KY = 128
NPIX = 16512
NGRP = 4
OR_G = 4
NCLS = 2
T_OFF = 5
RADIUS = 3
NCTF = 16
BLK = 2
NB = 4
SIG = 1
CAP = 2
PTOT = 128
NBLK = 64


def model_references(key):
    ref_key = jax.random.fold_in(key, 101)
    sorted_key_values = jax.random.fold_in(ref_key, 0)
    ref_shape = (NCLS, NGRP, OR_G, 2, NPIX)
    values = jax.random.normal(sorted_key_values, ref_shape, jnp.float32)
    return jnp.clip(values, -4.0, 4.0)


def model_offsets(key):
    side_count = 2 * RADIUS + 1
    picked = jax.random.permutation(jax.random.fold_in(key, 202), side_count * side_count)[:T_OFF].astype(jnp.int32)
    return jnp.stack([picked % side_count - RADIUS, picked // side_count - RADIUS], axis=1)


def draw_references(key, part):
    return model_references(key).astype(jnp.bfloat16)


def draw_offsets(key, part):
    return model_offsets(key)


def draw_particles(key, part):
    model_refs = model_references(key)
    shifts = model_offsets(key)
    pick_keys = jax.random.split(jax.random.fold_in(key, 303), 5)
    class_pick = jax.random.randint(pick_keys[0], (PTOT,), 0, NCLS)
    group_pick = jax.random.randint(pick_keys[1], (PTOT,), 0, NGRP)
    orient_pick = jax.random.randint(pick_keys[2], (PTOT,), 0, OR_G)
    shift_pick = jax.random.randint(pick_keys[3], (PTOT,), 0, T_OFF)
    chosen = model_refs[class_pick, group_pick, orient_pick]
    true_shift = shifts[shift_pick]
    pixel_index = jnp.arange(NPIX, dtype=jnp.int32)
    freq_x = pixel_index % KX
    freq_y = pixel_index // KX - KY // 2
    phase_rotations = jnp.mod(true_shift[:, 0:1] * freq_x[None, :] + true_shift[:, 1:2] * freq_y[None, :], BOX)
    angles = phase_rotations.astype(jnp.float32) * (2.0 * math.pi / BOX)
    cosines = jnp.cos(angles)
    sines = jnp.sin(angles)
    real_part = chosen[:, 0] * cosines + chosen[:, 1] * sines
    imag_part = chosen[:, 1] * cosines - chosen[:, 0] * sines
    signal = jnp.stack([real_part, imag_part], axis=1)
    noise_part = jnp.clip(jax.random.normal(pick_keys[4], (PTOT, 2, NPIX), jnp.float32), -4.0, 4.0)
    return (signal + noise_part).astype(jnp.bfloat16)


def place_ends(values, stream_key, low, largest):
    shape = values.shape
    spot = [jax.random.randint(jax.random.fold_in(stream_key, axis), (), 0, shape[axis]) for axis in range(len(shape))]
    values = values.at[tuple(spot)].set(low)
    longest = shape.index(max(shape))
    spot[longest] = (spot[longest] + 1) % shape[longest]
    return values.at[tuple(spot)].set(largest)


def levels(own_key, shape, cuts, least, top_value):
    def one(position, blocks):
        heights = jax.random.uniform(jax.random.fold_in(jax.random.fold_in(own_key, 6), position), (blocks,), jnp.float32, least / len(cuts), top_value / len(cuts))
        return jnp.repeat(jnp.exp(heights), shape[position] // blocks).reshape((-1,) + (1,) * (len(shape) - position - 1))

    loudness = one(*cuts[0])
    for cut in cuts[1:]:
        loudness = loudness * one(*cut)
    return loudness


def routed_block(own_key, own, number, rows, count, top, bound, lean):
    sequence = jax.random.permutation(own_key, count)
    packed, ordinary = load_shares(count, rows * top, bound, lean, True), load_shares(count, rows * top, bound, lean, False)
    places = jnp.arange(count)

    def named(tallies, offset_by):
        used = int((tallies > 0).sum())
        fixed = max(1, used // 4)
        passed = fixed + (places - fixed + offset_by * (used - fixed)) % max(1, count - fixed)
        return jnp.zeros((count,), jnp.int32).at[sequence[jnp.where(places < fixed, places, passed)]].set(jnp.asarray(tallies, jnp.int32))

    tallies = jnp.where(number % 4 == 0, named(packed, number // 4), named(ordinary, number - number // 4 - 1))
    mixed = jax.random.permutation(jax.random.fold_in(own, 3), count)
    giver, sink = mixed[0:count // 2 * 2:2], mixed[1:count // 2 * 2:2]
    slack = jnp.minimum(tallies[giver] - 1, bound - tallies[sink]) // 2
    slack = jnp.where((giver == sequence[0]) | (sink == sequence[0]) | (tallies[sink] == 0), 0, jnp.maximum(slack, 0))
    passed = jax.random.randint(jax.random.fold_in(own, 4), (count // 2,), 0, 1 << 20) % (slack + 1)
    tallies = tallies.at[giver].add(-passed).at[sink].add(passed)
    members = jnp.searchsorted(jnp.cumsum(tallies), jnp.arange(rows * top), side="right").astype(jnp.int32)
    grid = members.reshape(top, rows).T
    grid = grid[jax.random.permutation(jax.random.fold_in(own, 1), rows)]
    offset_by = jax.random.randint(jax.random.fold_in(own, 2), (rows, 1), 0, top)
    return jnp.take_along_axis(grid, (jnp.arange(top)[None, :] + offset_by) % top, axis=1)


def load_shares(count, total, reach, skew, full):
    portions = [(1 << 20) // math.isqrt(grade ** skew) + 1 for grade in range(1, count + 1)]
    largest = reach if full else min(reach, max(-(-total // count), total * portions[0] // sum(portions)))
    least = 1 if total - largest >= count - 1 else 0
    given, spare = [largest] + [least] * (count - 1), total - largest - least * (count - 1)
    while spare > 0:
        free = [i for i in range(1, count) if given[i] < largest] or [i for i in range(1, count) if given[i] < reach]
        pool, budget = sum([portions[i] for i in free]), spare
        for i in free:
            more = min(reach - given[i], max(1, budget * portions[i] // pool), spare)
            given[i] = given[i] + more
            spare = spare - more
    return np.array(given)


def setup_inputs(seed: int = 0, part: int = 0) -> dict:
    key_of = jax.random.split(jax.random.key(seed), 8)
    part_splits = jax.random.split(jax.random.fold_in(key_of[7], part), 8)
    particles = draw_particles(jax.random.fold_in(jax.random.fold_in(key_of[7], part), 71), part)
    ctf_index = place_ends(jax.random.randint(part_splits[1], (PTOT,), 0, NCTF), jax.random.fold_in(part_splits[1], 1), 0, NCTF - 1).astype(jnp.int32)
    beta = jnp.clip(jnp.exp(math.log(60.0) - 1.7917595 * jax.random.uniform(part_splits[2], (PTOT,), jnp.float32) ** levels(part_splits[2], (PTOT,), ((0, 16),), -0.2, 0.2)), 10.0, 60.0).astype(jnp.bfloat16)
    significant_keys = jax.random.split(jax.random.fold_in(part_splits[3], 1), NBLK // NB)
    significant_turns = jax.random.permutation(jax.random.fold_in(part_splits[3], 3), NBLK // NB)
    significant = jax.vmap(lambda own, number: routed_block(jax.random.fold_in(part_splits[3], 2), own, number, NB, NGRP, SIG, CAP, 3))(significant_keys, significant_turns).reshape((NBLK, SIG))
    ctf_table = jnp.clip(jax.random.uniform(key_of[4], (NCTF, NPIX), jnp.float32, 0.049804688, 1.0), 0.049804688, 1.0).astype(jnp.bfloat16)
    references = draw_references(jax.random.fold_in(jax.random.fold_in(key_of[7], part), 71), part)
    offsets = draw_offsets(jax.random.fold_in(jax.random.fold_in(key_of[7], part), 71), part)
    return {"particles": particles, "ctf_index": ctf_index, "beta": beta, "significant": significant, "ctf_table": ctf_table, "references": references, "offsets": offsets}


EPSILON = 1e-06

def phase_tables(offsets):
    pixel_index = jnp.arange(KX * KY, dtype=jnp.int32)
    freq_x = pixel_index % KX
    freq_y = pixel_index // KX - KY // 2
    phase_rotations = jnp.mod(offsets[:, 0:1] * freq_x[None, :] + offsets[:, 1:2] * freq_y[None, :], BOX)
    angles = phase_rotations.astype(jnp.float32) * (2.0 * math.pi / BOX)
    return (jnp.cos(angles), jnp.sin(angles))

def shifted_table(refs_now, cosines, sines):
    real_part = refs_now[:, 0, :].astype(jnp.float32)
    imag_part = refs_now[:, 1, :].astype(jnp.float32)
    translation_real = real_part[None] * cosines[:, None] + imag_part[None] * sines[:, None]
    shift_imag = imag_part[None] * cosines[:, None] - real_part[None] * sines[:, None]
    shifted = jnp.stack([translation_real, shift_imag], axis=2).astype(jnp.bfloat16)
    return shifted.reshape(shifted.shape[0] * shifted.shape[1], 2 * shifted.shape[3])

def ref_energy(refs_now):
    return lax.optimization_barrier(jnp.sum(jnp.square(refs_now.astype(jnp.float32)), axis=1))

def reference(particles, ctf_index, beta, significant, ctf_table, references, offsets):
    cosines, sines = phase_tables(offsets)
    ctf_rows = jnp.take(ctf_table, ctf_index, axis=0)
    particle_images = particles.astype(jnp.float32)
    weighted = (ctf_rows.astype(jnp.float32)[:, None, :] * particle_images).astype(jnp.bfloat16).reshape(PTOT, 2 * NPIX)
    image_power = lax.optimization_barrier(jnp.sum(particle_images * particle_images, axis=(1, 2)))
    ctf_squares = jnp.square(ctf_rows.astype(jnp.float32))
    inverse_noise = beta.astype(jnp.float32)
    block_of = jnp.arange(PTOT, dtype=jnp.int32) // BLK
    listed = jnp.any(significant[:, :, None] == jnp.arange(NGRP, dtype=jnp.int32)[None, None, :], axis=1).astype(jnp.float32)
    member_entry = jnp.take(listed, block_of, axis=0)

    def per_group(group_id):

        def per_class(class_id):
            refs_now = references[class_id, group_id]
            shifted = shifted_table(refs_now, cosines, sines)
            intersection = lax.dot_general(weighted, shifted, (((1,), (1,)), ((), ())), preferred_element_type=jnp.float32)
            energy = ref_energy(refs_now)
            ref_power = lax.dot_general(ctf_squares, energy, (((1,), (1,)), ((), ())), precision=lax.Precision.HIGHEST, preferred_element_type=jnp.float32)
            intersection = intersection.reshape(PTOT, T_OFF, OR_G)
            normalizer = jnp.sqrt(image_power[:, None] * ref_power + EPSILON)
            logits = inverse_noise[:, None, None] * intersection / normalizer[:, None, :]
            return lax.optimization_barrier(jnp.sum(jnp.exp(logits), axis=(1, 2)))
        return lax.map(per_class, jnp.arange(NCLS, dtype=jnp.int32))
    grouped_rows = lax.map(per_group, jnp.arange(NGRP, dtype=jnp.int32))
    marginal_evidence = jnp.einsum('ysm,my->ms', grouped_rows, member_entry, precision=lax.Precision.HIGHEST)
    all_classes = lax.optimization_barrier(jnp.sum(marginal_evidence, axis=1))
    return (marginal_evidence / all_classes[:, None], jnp.log(all_classes))
```

```python
import functools
import math

import jax
import jax.numpy as jnp
from jax import lax
from jax.experimental import pallas as pl
from jax.experimental.pallas import tpu as pltpu
from jax.sharding import PartitionSpec as P

BOX = 256
KX = 129
KY = 128

EPSILON = 1e-06
LANES = 128
SET = 4


def phase_tables(offsets):
    pixel_index = jnp.arange(KX * KY, dtype=jnp.int32)
    freq_x = pixel_index % KX
    freq_y = pixel_index // KX - KY // 2
    phase_rotations = jnp.mod(
        offsets[:, 0:1] * freq_x[None, :] + offsets[:, 1:2] * freq_y[None, :], BOX
    )
    angles = phase_rotations.astype(jnp.float32) * (2.0 * math.pi / BOX)
    return (jnp.cos(angles), jnp.sin(angles))


def tiled(values):
    rows, parts, pixels = values.shape
    split = values.reshape(rows, parts, pixels // LANES, LANES)
    return jnp.transpose(split, (0, 2, 1, 3))


def evidence_kernel(dims, *refs):
    n_img, n_full, rows, oris, tiles, shifts, codes, sig = dims
    refs = list(refs)
    gids = refs.pop(0)
    meta = refs.pop(0)
    ctf, cosines, sines = refs.pop(0), refs.pop(0), refs.pop(0)
    images = [refs.pop(0) for _ in range(n_img)]
    full = [refs.pop(0) for _ in range(n_full)]
    halves = [refs.pop(0) for _ in range(2)]
    outs = [refs.pop(0) for _ in range(n_img)]
    img_buf, ref_buf, ctf_rows, lhs, rhs, img_sem, ref_sem = refs

    pair = 2 * rows
    chunk_rows = 2 * oris
    chunk_pad = rhs.shape[0] // SET
    n_chunks = n_full + 1
    w_rows = n_img * pair

    def image_copies(i):
        return [
            pltpu.make_async_copy(images[i].at[p], img_buf.at[i, :, p], img_sem.at[i])
            for p in range(rows)
        ]

    def chunk_copies(c):
        if c < n_full:
            sources = [full[c].at[o] for o in range(oris)]
        else:
            half = oris // 2
            sources = [halves[o // half].at[o % half] for o in range(oris)]
        slot = c % SET
        return [
            pltpu.make_async_copy(sources[o], ref_buf.at[slot, :, o], ref_sem.at[slot])
            for o in range(oris)
        ]

    for i in range(n_img):
        for copy in image_copies(i):
            copy.start()
    for c in range(min(SET, n_chunks)):
        for copy in chunk_copies(c):
            copy.start()

    def lane(k):
        return pl.ds(pl.multiple_of(k * LANES, LANES), LANES)

    def square_step(k, carry):
        value = ctf[:, lane(k)].astype(jnp.float32)
        square = value * value
        high = square.astype(jnp.bfloat16)
        lhs[w_rows : w_rows + codes, lane(k)] = high
        lhs[w_rows + codes : w_rows + 2 * codes, lane(k)] = (
            square - high.astype(jnp.float32)
        ).astype(jnp.bfloat16)
        return carry

    lax.fori_loop(0, tiles, square_step, 0, unroll=3)

    code_ids = lax.broadcasted_iota(jnp.int32, (1, codes), 1).astype(jnp.float32)
    powers = []
    for i in range(n_img):
        span = slice(i * pair, (i + 1) * pair)
        pick = (meta[span, 0:1] == code_ids).astype(jnp.bfloat16)
        ctf_rows[...] = jnp.dot(pick, ctf[...], preferred_element_type=jnp.float32)
        for copy in image_copies(i):
            copy.wait()

        def weigh(k, total, i=i, span=span):
            value = img_buf[i, k].reshape(pair, LANES).astype(jnp.float32)
            lhs[span, lane(k)] = (ctf_rows[:, lane(k)] * value).astype(jnp.bfloat16)
            return total + value * value

        total = lax.fori_loop(
            0, tiles, weigh, jnp.zeros((pair, LANES), jnp.float32), unroll=3
        )
        powers.append(jnp.sum(total, axis=1, keepdims=True))
    power = jnp.concatenate(powers, axis=0)
    power = power + pltpu.roll(jnp.broadcast_to(power, (w_rows, LANES)), w_rows - 1, 0)[
        :, 0:1
    ]
    beta = meta[:, 1:2]
    pick_all = (meta[:, 0:1] == code_ids).astype(jnp.float32)
    pick_all = jnp.concatenate([pick_all, pick_all], axis=1)

    columns = rhs.shape[0]
    row_id = lax.broadcasted_iota(jnp.int32, (w_rows, columns), 0)
    col_id = lax.broadcasted_iota(jnp.int32, (w_rows, columns), 1)
    within = col_id % chunk_pad
    same_part = (row_id % 2) == (col_id % 2)
    odd = lax.broadcasted_iota(jnp.int32, (chunk_rows, LANES), 0) % 2 == 1

    evidence = jnp.zeros((w_rows, 1), jnp.float32)
    for first in range(0, n_chunks, SET):
        live = min(SET, n_chunks - first)
        for c in range(first, first + live):
            if first:
                for copy in chunk_copies(c):
                    copy.start()
        for c in range(first, first + live):
            for copy in chunk_copies(c):
                copy.wait()

        def shift_step(k, carry, live=live):
            cos = [cosines[t : t + 1, lane(k)] for t in range(shifts)]
            sin = [sines[t : t + 1, lane(k)] for t in range(shifts)]
            for slot in range(live):
                value = ref_buf[slot, k].reshape(chunk_rows, LANES).astype(jnp.float32)
                turned = jnp.where(
                    odd,
                    -pltpu.roll(value, 1, 0),
                    pltpu.roll(value, chunk_rows - 1, 0),
                )
                parts = [value * cos[t] + turned * sin[t] for t in range(shifts)]
                square = value * value
                high = square.astype(jnp.bfloat16).astype(jnp.float32)
                parts += [high, square - high]
                spare = chunk_pad - len(parts) * chunk_rows
                if spare:
                    parts.append(jnp.zeros((spare, LANES), jnp.float32))
                rhs[slot * chunk_pad : (slot + 1) * chunk_pad, lane(k)] = jnp.concatenate(
                    parts, axis=0
                ).astype(jnp.bfloat16)
            return carry

        lax.fori_loop(0, tiles, shift_step, 0)
        product = lax.dot_general(
            lhs[...], rhs[...], (((1,), (1,)), ((), ())), preferred_element_type=jnp.float32
        )
        cross = jnp.where(same_part, product[:w_rows], 0.0)
        cross = cross + pltpu.roll(cross, w_rows - 1, 0)
        cross = cross + pltpu.roll(cross, columns - 1, 1)
        energy = jnp.dot(
            pick_all,
            product[w_rows:],
            precision=lax.Precision.HIGHEST,
            preferred_element_type=jnp.float32,
        )
        energy = energy + pltpu.roll(energy, columns - chunk_rows, 1)
        energy = energy + pltpu.roll(energy, columns - 1, 1)
        spread = jnp.zeros_like(energy)
        for t in range(shifts):
            moved = pltpu.roll(energy, columns - (shifts - t) * chunk_rows, 1)
            spread = jnp.where(within // chunk_rows == t, moved, spread)
        wanted = (within < shifts * chunk_rows) & (col_id % 2 == 0)
        named = jnp.zeros((w_rows, columns), jnp.bool_)
        for slot in range(live):
            gid = gids[first + slot]
            for s in range(sig):
                hit = meta[:, 2 + s : 3 + s].astype(jnp.int32) == gid
                named = named | (hit & (col_id // chunk_pad == slot))
        wanted = wanted & named & (row_id % 2 == 0)
        normalizer = jnp.sqrt(power * spread + EPSILON)
        logits = jnp.where(wanted, beta * cross / jnp.where(wanted, normalizer, 1.0), 0.0)
        evidence = evidence + jnp.sum(
            jnp.where(wanted, jnp.exp(logits), 0.0), axis=1, keepdims=True
        )
    particle = lax.broadcasted_iota(jnp.int32, (w_rows, LANES), 0)
    place = lax.broadcasted_iota(jnp.int32, (w_rows, LANES), 1)
    for i in range(n_img):
        chosen = (particle == i * pair + 2 * place) & (place < rows)
        outs[i][...] = jnp.sum(jnp.where(chosen, evidence, 0.0), axis=0, keepdims=True)


def finish_kernel(rows, me, *refs):
    n_cls = len(refs) - 2
    post, log_out = refs[-2:]
    x = me[0]
    own = [r[...] for r in refs[:n_cls]]
    total = own[0]
    for value in own[1:]:
        total = total + value
    row = lax.broadcasted_iota(jnp.int32, (n_cls, LANES), 0)
    table = jnp.zeros((n_cls, LANES), jnp.float32)
    for k in range(n_cls):
        table = jnp.where(row == (x ^ k), own[k], table)
    post[...] = (table / total)[:, :rows]
    log_out[...] = jnp.log(total)[:, :rows]


def local(particles, ctf_index, beta, significant, ctf_table, references, offsets):
    groups = lax.axis_size("orient")
    n_cls = lax.axis_size("cls")
    cores = lax.axis_size("dom")
    blocks, sig = significant.shape
    rows, _, pixels = particles.shape
    per_block = rows // blocks
    codes = ctf_table.shape[0]
    oris = references.shape[2]
    shifts = offsets.shape[0]
    tiles = pixels // LANES
    refs_own = references.reshape(oris, 2, pixels)
    z = lax.axis_index("orient")
    x = lax.axis_index("cls")
    d = lax.axis_index("dom")
    steps = list(range(1, groups))

    def core_step(first, second):
        pairs = []
        for a in range(groups):
            for core in range(cores):
                step = second if core else first
                pairs.append((a * cores + core, (a ^ step) * cores + core))
        return pairs

    swap = [(c, cores - 1 - c) for c in range(cores)]
    direct, order = [], []
    while len(steps) > 1:
        first, second = steps.pop(0), steps.pop(0)
        direct.append(lax.ppermute(refs_own, ("orient", "dom"), core_step(first, second)))
        order.append((first, second))

    def across(values, k):
        return lax.ppermute(values, "cls", [(c, c ^ k) for c in range(n_cls)])

    images = [particles] + [across(particles, k) for k in range(1, n_cls)]
    last = steps.pop(0)
    half = oris // 2
    part = lax.dynamic_slice_in_dim(refs_own, d * half, half, axis=0)
    near_half = lax.ppermute(part, "orient", [(a, a ^ last) for a in range(groups)])
    own_meta = jnp.concatenate(
        [
            ctf_index.astype(jnp.float32)[:, None],
            beta.astype(jnp.float32)[:, None],
            jnp.repeat(significant.astype(jnp.float32), per_block, axis=0),
        ],
        axis=1,
    )
    metas = [own_meta] + [across(own_meta, k) for k in range(1, n_cls)]
    meta = jnp.repeat(jnp.concatenate(metas, axis=0), 2, axis=0)
    cosines, sines = phase_tables(offsets)
    mates = [lax.ppermute(values, "dom", swap) for values in direct]
    far_half = lax.ppermute(near_half, "dom", swap)

    chunks, ids = [refs_own], [z]
    for (first, second), near, mate in zip(order, direct, mates):
        chunks += [near, mate]
        ids += [z ^ jnp.where(d == 0, first, second), z ^ jnp.where(d == 0, second, first)]
    ids.append(z ^ last)
    gids = jnp.stack(ids).astype(jnp.int32)

    n_img = len(images)
    chunk_pad = -(-(shifts + 2) * 2 * oris // 16) * 16
    dims = (n_img, len(chunks), rows, oris, tiles, shifts, codes, sig)
    anywhere = pl.BlockSpec(memory_space=pl.ANY)
    vmem = pl.BlockSpec(memory_space=pltpu.VMEM)
    smem = pl.BlockSpec(memory_space=pltpu.SMEM)
    evidence = pl.pallas_call(
        functools.partial(evidence_kernel, dims),
        name="evidence",
        out_shape=[jax.ShapeDtypeStruct((1, LANES), jnp.float32)] * n_img,
        in_specs=[smem, vmem, vmem, vmem, vmem] + [anywhere] * (n_img + len(chunks) + 2),
        out_specs=[vmem] * n_img,
        scratch_shapes=[
            pltpu.VMEM((n_img, tiles, rows, 2, LANES), jnp.bfloat16),
            pltpu.VMEM((SET, tiles, oris, 2, LANES), jnp.bfloat16),
            pltpu.VMEM((2 * rows, pixels), jnp.float32),
            pltpu.VMEM((n_img * 2 * rows + 2 * codes, pixels), jnp.bfloat16),
            pltpu.VMEM((SET * chunk_pad, pixels), jnp.bfloat16),
            pltpu.SemaphoreType.DMA((n_img,)),
            pltpu.SemaphoreType.DMA((SET,)),
        ],
        compiler_params=pltpu.CompilerParams(vmem_limit_bytes=40 << 20),
    )(
        gids,
        meta,
        ctf_table,
        cosines,
        sines,
        *[tiled(v) for v in images],
        *[tiled(v) for v in chunks],
        tiled(near_half),
        tiled(far_half),
    )
    gathered = [evidence[0]] + [across(evidence[k], k) for k in range(1, n_cls)]
    post, log_total = pl.pallas_call(
        functools.partial(finish_kernel, rows),
        name="finish",
        out_shape=[
            jax.ShapeDtypeStruct((n_cls, rows), jnp.float32),
            jax.ShapeDtypeStruct((1, rows), jnp.float32),
        ],
        in_specs=[smem] + [vmem] * n_cls,
        out_specs=[vmem, vmem],
    )(x.astype(jnp.int32)[None], *gathered)
    return (post.T, log_total.reshape(rows))


def solution(mesh):
    placed = (
        P(("groups", "orient", "cls", "dom"), None, None),
        P(("groups", "orient", "cls", "dom")),
        P(("groups", "orient", "cls", "dom")),
        P(("groups", "orient", "cls", "dom"), None),
        P(),
        P(("groups", "cls"), "orient", None, None, None),
        P("groups", None),
    )
    return jax.shard_map(
        local,
        mesh=mesh,
        in_specs=placed,
        out_specs=(
            P(("groups", "orient", "cls", "dom"), None),
            P(("groups", "orient", "cls", "dom")),
        ),
        check_vma=False,
    )
```

```python
import functools
import math

import jax
import jax.numpy as jnp
from jax import lax
from jax.experimental import pallas as pl
from jax.experimental.pallas import tpu as pltpu
from jax.sharding import PartitionSpec as P


BOX = 256
KX = 129
KY = 128

EPSILON = 1e-06
LANES = 128
UNROLL = 43
SET = 4
F32 = jnp.float32
BF16 = jnp.bfloat16
CONTRACT_LAST = (((1,), (1,)), ((), ()))


def lane(k, width=LANES):
    return pl.ds(pl.multiple_of(k * width, LANES), width)


def iota(shape, axis):
    return lax.broadcasted_iota(jnp.int32, shape, axis)


def row_copies(source, target, sem, start=0):
    return [
        pltpu.make_async_copy(
            source.at[i], target.at[start + 2 * i : start + 2 * i + 2], sem
        )
        for i in range(source.shape[0])
    ]


def weigh_kernel(dims, codes_in, beta_in, groups_in, particles, ctf_in, refs, out, part,
                 codes, beta, groups, ctf, raw, rows_ctf, sem, half_sem, small_sem):
    rows, per_block, n_codes, tiles, sig = dims
    half = part.shape[0]
    small = [
        pltpu.make_async_copy(codes_in, codes, small_sem.at[0]),
        pltpu.make_async_copy(groups_in, groups, small_sem.at[1]),
        pltpu.make_async_copy(ctf_in, ctf, small_sem.at[2]),
        pltpu.make_async_copy(beta_in, beta, small_sem.at[3]),
    ]
    for copy in small:
        copy.start()
    copies = row_copies(particles, raw, sem)
    for copy in copies:
        copy.start()
    half_copy = pltpu.make_async_copy(refs.at[pl.ds(lax.axis_index("dom") * half, half)], part, half_sem)
    half_copy.start()
    shape = (2 * rows, LANES)
    owner = iota(shape, 0) // 2
    column = iota(shape, 1)
    for copy in small:
        copy.wait()
    noise = beta[...].astype(F32)
    noise = jnp.where(iota((2 * rows, rows), 0) // 2 == iota((2 * rows, rows), 1), noise, 0.0)
    extra = jnp.where(column == 1, jnp.sum(noise, axis=1, keepdims=True), 0.0)
    code = jnp.zeros(shape, jnp.int32)
    for p in range(rows):
        mine = owner == p
        code = jnp.where(mine, codes[p], code)
        for s in range(sig):
            group = groups[s, p // per_block].astype(F32)
            extra = jnp.where(mine & (column == 2 + s), group, extra)
    extra = jnp.where(column == 0, code.astype(F32), extra)
    pick = (code[:, :n_codes] == column[:, :n_codes]).astype(BF16)
    rows_ctf[...] = jnp.dot(pick, ctf[...], preferred_element_type=F32)
    for copy in copies:
        copy.wait()

    def step(k, power):
        value = raw[:, lane(k)].astype(F32)
        out[:, lane(k)] = (rows_ctf[:, lane(k)] * value).astype(BF16)
        return power + value * value

    power = lax.fori_loop(0, tiles, step, jnp.zeros(shape, F32), unroll=UNROLL)
    power = jnp.sum(power, axis=1, keepdims=True)
    for s in range(3):
        term = power.astype(BF16).astype(F32)
        extra = jnp.where(column == 2 + sig + s, term, extra)
        power = power - term
    out[:, tiles * LANES :] = extra.astype(BF16)
    half_copy.wait()


def up(value, to):
    return -(-value // to) * to


def prepare_kernel(tiles, images, ctf_in, offsets_in, lhs, cosines, sines, ctf, offsets, sem, small_sem):
    load = pltpu.make_async_copy(ctf_in, ctf, sem)
    load.start()
    small = pltpu.make_async_copy(offsets_in, offsets, small_sem)
    small.start()
    rows, codes = images.shape[0], ctf.shape[0]
    shape = cosines.shape[:1] + (LANES,)
    row, place = iota(shape, 0), iota(shape, 1)
    small.wait()
    step_x = jnp.zeros(shape, jnp.int32)
    step_y = jnp.zeros(shape, jnp.int32)
    for t in range(offsets.shape[1]):
        step_x = jnp.where(row == t, offsets[0, t], step_x)
        step_y = jnp.where(row == t, offsets[1, t], step_y)
    base = step_x * place - step_y * (KY // 2)
    slope = step_y - step_x
    wrapped = step_x * KX - step_y
    load.wait()

    def step(k, carry):
        lhs[:rows, lane(k)] = images[:, lane(k)]
        value = ctf[:, lane(k)].astype(F32)
        square = value * value
        high = square.astype(BF16)
        lhs[rows : rows + codes, lane(k)] = high
        lhs[rows + codes :, lane(k)] = (square - high.astype(F32)).astype(BF16)
        turn = (base + slope * k + jnp.where(place < k, wrapped, 0)) & (BOX - 1)
        quarter = (turn + BOX // 8) >> 6
        x = (turn - (quarter << 6)).astype(F32) * (2.0 * math.pi / BOX)
        x2 = x * x
        sin = x + x * x2 * (
            -1.6666654611e-1 + x2 * (8.3321608736e-3 + x2 * -1.9515295891e-4)
        )
        cos = (1.0 - 0.5 * x2) + x2 * x2 * (
            4.166664568298827e-2 + x2 * (-1.388731625493765e-3 + x2 * 2.443315711809948e-5)
        )
        swap = (quarter & 1) == 1
        first = jnp.where(swap, sin, cos)
        second = jnp.where(swap, cos, sin)
        cosines[:, lane(k)] = jnp.where(((quarter + 1) & 2) == 2, -first, first)
        sines[:, lane(k)] = jnp.where((quarter & 2) == 2, -second, second)
        return carry

    lax.fori_loop(0, tiles, step, 0, unroll=UNROLL)


def shift_rows(raw, cosines, sines, table, shifts, tiles):
    n = raw.shape[0]
    odd = iota((n, LANES), 0) % 2 == 1

    def step(k, carry):
        value = raw[:, lane(k)].astype(F32)
        turned = jnp.where(odd, -pltpu.roll(value, 1, 0), pltpu.roll(value, n - 1, 0))
        parts = [
            value * cosines[t : t + 1, lane(k)] + turned * sines[t : t + 1, lane(k)]
            for t in range(shifts)
        ]
        square = value * value
        high = square.astype(BF16).astype(F32)
        parts += [high, square - high]
        for i in range(0, len(parts), 2):
            both = jnp.concatenate(parts[i : i + 2], axis=0)
            table[n * i : n * i + both.shape[0], lane(k)] = both.astype(BF16)
        return carry

    lax.fori_loop(0, tiles, step, 0, unroll=UNROLL)


def tables_kernel(shifts, tiles, lhs, cosines, sines, *refs):
    pieces = refs[:-4]
    table, product, raw, sem = refs[-4:]
    n = raw.shape[0]
    copies = []
    for i, piece in enumerate(pieces):
        copies += row_copies(piece, raw, sem, i * n // len(pieces))
    for copy in copies:
        copy.start()
    for copy in copies:
        copy.wait()
    shift_rows(raw, cosines, sines, table, shifts, tiles)
    product[...] = lax.dot_general(
        table[...], lhs[...], CONTRACT_LAST, preferred_element_type=F32
    )


def last_kernel(dims, *refs):
    n_img, steps, shifts, tiles, sig, n = dims
    count = len(steps)
    refs = list(refs)
    z, d = lax.axis_index("orient"), lax.axis_index("dom")
    images = [refs.pop(0) for _ in range(n_img)]
    tables = [refs.pop(0) for _ in range(count)]
    products = [refs.pop(0) for _ in range(count)]
    outs = refs
    pixels = tiles * LANES
    rows = images[0].shape[0]
    codes = (products[0].shape[1] - rows) // 2
    total_rows = n_img * rows
    used = up(shifts * n, 16)

    others = []
    if n_img > 1:
        stacked = jnp.concatenate([table[:used, :] for table in tables], axis=0)
    for image in images[1:]:
        others.append(
            lax.dot_general(
                stacked, image[:, :pixels], CONTRACT_LAST, preferred_element_type=F32
            )
        )
    extra = jnp.concatenate([image[:, pixels:] for image in images], axis=0)
    take = (iota((16, LANES), 0) == iota((16, LANES), 1)).astype(BF16)
    turned = lax.dot_general(take, extra, CONTRACT_LAST, preferred_element_type=F32)
    beta = turned[1:2]
    power = turned[2 + sig : 3 + sig] + turned[3 + sig : 4 + sig] + turned[4 + sig : 5 + sig]
    power = power + pltpu.roll(power, total_rows - 1, 1)
    column = iota((total_rows, 6 * codes), 1)
    pick = (extra[:, 0:1].astype(F32).astype(jnp.int32) == column % codes).astype(BF16)
    squares = jnp.concatenate(
        [product[shifts * n : (shifts + 2) * n, rows:] for product in products], axis=0
    )
    terms = []
    for _ in range(3):
        term = squares.astype(BF16)
        terms.append(term)
        squares = squares - term.astype(F32)
    energies = lax.dot_general(
        jnp.concatenate(terms, axis=1), pick, CONTRACT_LAST, preferred_element_type=F32
    )

    even_row = iota((n, total_rows), 0) % 2 == 0
    same = (iota((n, total_rows), 0) % 2) == (iota((n, total_rows), 1) % 2)
    evidence = jnp.zeros((n, total_rows), F32)
    for c in range(count):
        energy = energies[2 * c * n : (2 * c + 1) * n] + energies[(2 * c + 1) * n : (2 * c + 2) * n]
        energy = energy + pltpu.roll(energy, n - 1, 0)
        scale = beta / jnp.sqrt(power * energy + EPSILON)
        cross = [products[c][: shifts * n, :rows]]
        cross += [other[c * used : c * used + shifts * n] for other in others]
        cross = jnp.concatenate(cross, axis=1) if len(cross) > 1 else cross[0]
        total = jnp.zeros((n, total_rows), F32)
        for t in range(shifts):
            value = jnp.where(same, cross[t * n : (t + 1) * n], 0.0)
            value = value + pltpu.roll(value, n - 1, 0)
            value = value + pltpu.roll(value, total_rows - 1, 1)
            total = total + jnp.exp(jnp.where(same & even_row, value * scale, 0.0))
        gid = (z ^ jnp.where(d == 0, *steps[c])).astype(F32)
        named = turned[2:3] == gid
        for s in range(1, sig):
            named = named | (turned[2 + s : 3 + s] == gid)
        evidence = evidence + jnp.where(even_row & named, total, 0.0)
    evidence = jnp.sum(evidence, axis=0, keepdims=True)
    spread = jnp.concatenate(
        [evidence, jnp.zeros((1, LANES - total_rows % LANES), F32)], axis=1
    ) if total_rows % LANES else evidence
    for i in range(n_img):
        here = spread if i == 0 else pltpu.roll(spread, LANES - i * rows, 1)
        outs[i][...] = jnp.where(iota((1, LANES), 1) < rows, here, 1.0)


def finish_kernel(rows, *refs):
    n_cls = len(refs) - 2
    post, log_out = refs[-2:]
    x = lax.axis_index("cls")
    place = iota((1, LANES), 1)
    used = (place % 2 == 0) & (place < 2 * rows)
    found = [jnp.where(used, r[...], 1.0) for r in refs[:n_cls]]
    total = found[0]
    for value in found[1:]:
        total = total + value
    row = iota((n_cls, LANES), 0)
    table = jnp.zeros((n_cls, LANES), F32)
    for k in range(n_cls):
        table = jnp.where(row == (x ^ k), found[k], table)
    squeeze = (iota((LANES, rows), 0) == 2 * iota((LANES, rows), 1)).astype(F32)
    both = jnp.concatenate([table / total, jnp.log(total)], axis=0)
    both = jnp.dot(both, squeeze, precision=lax.Precision.HIGHEST, preferred_element_type=F32)
    post[...] = both[:n_cls]
    log_out[...] = both[n_cls:]


def local(particles, ctf_index, beta, significant, ctf_table, references, offsets):
    groups = lax.axis_size("orient")
    n_cls = lax.axis_size("cls")
    cores = lax.axis_size("dom")
    blocks, sig = significant.shape
    rows, _, pixels = particles.shape
    per_block = rows // blocks
    codes = ctf_table.shape[0]
    oris = references.shape[2]
    shifts = offsets.shape[0]
    tiles = pixels // LANES
    refs_own = references.reshape(oris, 2, pixels)
    steps = list(range(1, groups))
    anywhere = pl.BlockSpec(memory_space=pl.ANY)
    vmem = pl.BlockSpec(memory_space=pltpu.VMEM)
    hbm = pl.BlockSpec(memory_space=pltpu.HBM)
    dma = pltpu.SemaphoreType.DMA

    def in_hbm(values):
        return pltpu.with_memory_space_constraint(values, pltpu.HBM)

    def core_step(first, second):
        pairs = []
        for a in range(groups):
            for core in range(cores):
                step = second if core else first
                pairs.append((a * cores + core, (a ^ step) * cores + core))
        return pairs

    swap = [(c, cores - 1 - c) for c in range(cores)]
    direct, order = [], []
    while len(steps) > 1:
        first, second = steps.pop(0), steps.pop(0)
        direct.append(
            lax.ppermute(refs_own, ("orient", "dom"), core_step(first, second))
        )
        order.append((first, second))
    last = steps.pop(0)

    def across(values, k):
        return lax.ppermute(values, "cls", [(c, c ^ k) for c in range(n_cls)])

    half = oris // 2
    weighted, part = pl.pallas_call(
        functools.partial(weigh_kernel, (rows, per_block, codes, tiles, sig)),
        name="weigh",
        out_shape=[
            jax.ShapeDtypeStruct((2 * rows, pixels + LANES), BF16),
            jax.ShapeDtypeStruct((half, 2, pixels), BF16),
        ],
        in_specs=[hbm, hbm, hbm, hbm, hbm, hbm],
        out_specs=[vmem, vmem],
        scratch_shapes=[
            pltpu.SMEM((rows,), jnp.int32),
            pltpu.VMEM((1, rows), BF16),
            pltpu.SMEM((sig, blocks), jnp.int32),
            pltpu.VMEM((codes, pixels), BF16),
            pltpu.VMEM((2 * rows, pixels), BF16),
            pltpu.VMEM((2 * rows, pixels), F32),
            dma,
            dma,
            dma((4,)),
        ],
        compiler_params=pltpu.CompilerParams(vmem_limit_bytes=16 << 20),
    )(
        in_hbm(ctf_index),
        in_hbm(beta[None]),
        in_hbm(significant.T),
        in_hbm(particles),
        in_hbm(ctf_table),
        in_hbm(refs_own),
    )
    images = [weighted]
    for k in range(1, n_cls):
        images.append(across(weighted, k))
    near_half = lax.ppermute(part, "orient", [(a, a ^ last) for a in range(groups)])
    lhs_rows = 2 * rows + 2 * codes
    phase_shape = jax.ShapeDtypeStruct((up(shifts, 8), pixels), F32)
    lhs, cosines, sines = pl.pallas_call(
        functools.partial(prepare_kernel, tiles),
        name="prepare",
        out_shape=[
            jax.ShapeDtypeStruct((lhs_rows, pixels), BF16),
            phase_shape,
            phase_shape,
        ],
        in_specs=[vmem, hbm, hbm],
        out_specs=[vmem, vmem, vmem],
        scratch_shapes=[
            pltpu.VMEM((codes, pixels), BF16),
            pltpu.SMEM((2, shifts), jnp.int32),
            dma,
            dma,
        ],
        compiler_params=pltpu.CompilerParams(vmem_limit_bytes=16 << 20),
    )(weighted, in_hbm(ctf_table), in_hbm(offsets.T))
    n = 2 * oris
    n_img = len(images)

    used = (shifts + 2) * n

    def make_table(*pieces):
        return pl.pallas_call(
            functools.partial(tables_kernel, shifts, tiles),
            name="tables",
            out_shape=[
                jax.ShapeDtypeStruct((used, pixels), BF16),
                jax.ShapeDtypeStruct((used, lhs_rows), F32),
            ],
            in_specs=[vmem, vmem, vmem] + [anywhere] * len(pieces),
            out_specs=[vmem, vmem],
            scratch_shapes=[pltpu.VMEM((n, pixels), BF16), dma],
            compiler_params=pltpu.CompilerParams(vmem_limit_bytes=12 << 20),
        )(lhs, cosines, sines, *pieces)

    def evaluate(group):
        steps, tables, products = zip(*group)
        return pl.pallas_call(
            functools.partial(last_kernel, (n_img, steps, shifts, tiles, sig, n)),
            name="last",
            out_shape=[jax.ShapeDtypeStruct((1, LANES), F32)] * n_img,
            in_specs=[vmem] * (n_img + 2 * len(group)),
            out_specs=[vmem] * n_img,
            compiler_params=pltpu.CompilerParams(
                vmem_limit_bytes=(12 << 20) if n_img < 4 else (40 << 20)
            ),
        )(*images, *tables, *products)

    made = [((0, 0), *make_table(in_hbm(refs_own)))]
    for (first, second), near in zip(order, direct):
        mate = lax.ppermute(near, "dom", swap)
        made.append(((first, second), *make_table(near)))
        made.append(((second, first), *make_table(mate)))
    far_half = lax.ppermute(near_half, "dom", swap)
    made.append(((last, last), *make_table(near_half, far_half)))
    found = [evaluate(made[i : i + SET]) for i in range(0, len(made), SET)]
    evidence = found[0]
    for more in found[1:]:
        evidence = [a + b for a, b in zip(evidence, more)]
    gathered = [evidence[0]] + [across(evidence[k], k) for k in range(1, n_cls)]
    post, log_total = pl.pallas_call(
        functools.partial(finish_kernel, rows),
        name="finish",
        out_shape=[
            jax.ShapeDtypeStruct((n_cls, rows), F32),
            jax.ShapeDtypeStruct((1, rows), F32),
        ],
        in_specs=[vmem] * n_cls,
        out_specs=[vmem, vmem],
        compiler_params=pltpu.CompilerParams(vmem_limit_bytes=8 << 20),
    )(*gathered)
    return (post.T, log_total.reshape(rows))


def solution(mesh):
    placed = (
        P(("groups", "orient", "cls", "dom"), None, None),
        P(("groups", "orient", "cls", "dom")),
        P(("groups", "orient", "cls", "dom")),
        P(("groups", "orient", "cls", "dom"), None),
        P(),
        P(("groups", "cls"), "orient", None, None, None),
        P("groups", None),
    )

    return jax.shard_map(
        local,
        mesh=mesh,
        in_specs=placed,
        out_specs=(
            P(("groups", "orient", "cls", "dom"), None),
            P(("groups", "orient", "cls", "dom")),
        ),
        check_vma=False,
    )
```

```python
import functools
import math

import jax
import jax.numpy as jnp
from jax import lax
from jax.experimental import pallas as pl
from jax.experimental.pallas import tpu as pltpu
from jax.sharding import PartitionSpec as P


BOX = 256
KX = 129
KY = 128

EPSILON = 1e-06
LANES = 128
UNROLL = 43
SET = 4
F32 = jnp.float32
BF16 = jnp.bfloat16
CONTRACT_LAST = (((1,), (1,)), ((), ()))


def lane(k, width=LANES):
    return pl.ds(pl.multiple_of(k * width, LANES), width)


def iota(shape, axis):
    return lax.broadcasted_iota(jnp.int32, shape, axis)


def row_copies(source, target, sem, start=0):
    return [
        pltpu.make_async_copy(
            source.at[i], target.at[start + 2 * i : start + 2 * i + 2], sem
        )
        for i in range(source.shape[0])
    ]


def weigh_kernel(dims, codes_in, beta_in, groups_in, particles, ctf_in, refs, first, rest, part, ctf,
                 codes, beta, groups, raw, sem, ctf_sem, half_sem, small_sem):
    rows, per_block, n_codes, sig = dims
    half = part.shape[0]
    small = [
        pltpu.make_async_copy(codes_in, codes, small_sem.at[0]),
        pltpu.make_async_copy(groups_in, groups, small_sem.at[1]),
        pltpu.make_async_copy(beta_in, beta, small_sem.at[2]),
    ]
    for copy in small:
        copy.start()
    cut, pixels = first.shape[1], raw.shape[1]
    spans = (slice(0, cut), slice(cut, pixels))
    loads = []
    for b, span in enumerate(spans):
        copies = [pltpu.make_async_copy(ctf_in.at[:, span], ctf.at[:, span], ctf_sem.at[b])]
        for p in range(rows):
            copies.append(
                pltpu.make_async_copy(
                    particles.at[p, :, span], raw.at[2 * p : 2 * p + 2, span], sem.at[b]
                )
            )
        loads.append(copies)
        for copy in copies:
            copy.start()
    half_copy = pltpu.make_async_copy(
        refs.at[pl.ds(lax.axis_index("dom") * half, half)], part, half_sem
    )
    half_copy.start()
    shape = (2 * rows, LANES)
    owner = iota(shape, 0) // 2
    column = iota(shape, 1)
    for copy in small:
        copy.wait()
    noise = beta[...].astype(F32)
    noise = jnp.where(iota((2 * rows, rows), 0) // 2 == iota((2 * rows, rows), 1), noise, 0.0)
    extra = jnp.where(column == 1, jnp.sum(noise, axis=1, keepdims=True), 0.0)
    code = jnp.zeros(shape, jnp.int32)
    for p in range(rows):
        mine = owner == p
        code = jnp.where(mine, codes[p], code)
        for s in range(sig):
            group = groups[s, p // per_block].astype(F32)
            extra = jnp.where(mine & (column == 2 + s), group, extra)
    extra = jnp.where(column == 0, code.astype(F32), extra)
    pick = (code[:, :n_codes] == column[:, :n_codes]).astype(BF16)
    power = jnp.zeros((2 * rows, 1), F32)
    for copies, span, out in zip(loads, spans, (first, rest)):
        for copy in copies:
            copy.wait()
        value = raw[:, span].astype(F32)
        chosen = jnp.dot(pick, ctf[:, span], preferred_element_type=F32)
        out[:, : span.stop - span.start] = (chosen * value).astype(BF16)
        power = power + jnp.sum(value * value, axis=1, keepdims=True)
    for s in range(3):
        term = power.astype(BF16).astype(F32)
        extra = jnp.where(column == 2 + sig + s, term, extra)
        power = power - term
    rest[:, pixels - cut :] = extra.astype(BF16)
    half_copy.wait()


def up(value, to):
    return -(-value // to) * to


def prepare_kernel(tiles, first, rest, ctf, offsets_in, refs, lhs, cosines, sines, table, product, raw, offsets, sem, small_sem):
    copies = row_copies(refs, raw, sem)
    for copy in copies:
        copy.start()
    small = pltpu.make_async_copy(offsets_in, offsets, small_sem)
    small.start()
    rows, codes = first.shape[0], ctf.shape[0]
    cut = first.shape[1]
    lhs[:rows, :cut] = first[...]
    lhs[:rows, cut:] = rest[:, : lhs.shape[1] - cut]
    shape = cosines.shape[:1] + (LANES,)
    row, place = iota(shape, 0), iota(shape, 1)
    small.wait()
    step_x = jnp.zeros(shape, jnp.int32)
    step_y = jnp.zeros(shape, jnp.int32)
    for t in range(offsets.shape[1]):
        step_x = jnp.where(row == t, offsets[0, t], step_x)
        step_y = jnp.where(row == t, offsets[1, t], step_y)
    base = step_x * place - step_y * (KY // 2)
    slope = step_y - step_x
    wrapped = step_x * KX - step_y

    def step(k, carry):
        value = ctf[:, lane(k)].astype(F32)
        square = value * value
        high = square.astype(BF16)
        lhs[rows : rows + codes, lane(k)] = high
        lhs[rows + codes :, lane(k)] = (square - high.astype(F32)).astype(BF16)
        turn = (base + slope * k + jnp.where(place < k, wrapped, 0)) & (BOX - 1)
        quarter = (turn + BOX // 8) >> 6
        x = (turn - (quarter << 6)).astype(F32) * (2.0 * math.pi / BOX)
        x2 = x * x
        sin = x + x * x2 * (
            -1.6666654611e-1 + x2 * (8.3321608736e-3 + x2 * -1.9515295891e-4)
        )
        cos = (1.0 - 0.5 * x2) + x2 * x2 * (
            4.166664568298827e-2 + x2 * (-1.388731625493765e-3 + x2 * 2.443315711809948e-5)
        )
        swap = (quarter & 1) == 1
        first = jnp.where(swap, sin, cos)
        second = jnp.where(swap, cos, sin)
        cosines[:, lane(k)] = jnp.where(((quarter + 1) & 2) == 2, -first, first)
        sines[:, lane(k)] = jnp.where((quarter & 2) == 2, -second, second)
        return carry

    lax.fori_loop(0, tiles, step, 0, unroll=UNROLL)
    for copy in copies:
        copy.wait()
    shift_rows(raw, cosines, sines, table, offsets.shape[1], tiles)
    product[...] = lax.dot_general(
        table[...], lhs[...], CONTRACT_LAST, preferred_element_type=F32
    )


def shift_rows(raw, cosines, sines, table, shifts, tiles):
    n = raw.shape[0]
    odd = iota((n, LANES), 0) % 2 == 1

    def step(k, carry):
        value = raw[:, lane(k)].astype(F32)
        turned = jnp.where(odd, -pltpu.roll(value, 1, 0), pltpu.roll(value, n - 1, 0))
        parts = [
            value * cosines[t : t + 1, lane(k)] + turned * sines[t : t + 1, lane(k)]
            for t in range(shifts)
        ]
        square = value * value
        high = square.astype(BF16).astype(F32)
        parts += [high, square - high]
        for i in range(0, len(parts), 2):
            both = jnp.concatenate(parts[i : i + 2], axis=0)
            table[n * i : n * i + both.shape[0], lane(k)] = both.astype(BF16)
        return carry

    lax.fori_loop(0, tiles, step, 0, unroll=UNROLL)


def tables_kernel(shifts, tiles, lhs, cosines, sines, *refs):
    pieces = refs[:-4]
    table, product, raw, sem = refs[-4:]
    n = raw.shape[0]
    copies = []
    for i, piece in enumerate(pieces):
        copies += row_copies(piece, raw, sem, i * n // len(pieces))
    for copy in copies:
        copy.start()
    for copy in copies:
        copy.wait()
    shift_rows(raw, cosines, sines, table, shifts, tiles)
    product[...] = lax.dot_general(
        table[...], lhs[...], CONTRACT_LAST, preferred_element_type=F32
    )


def against(tables, used, span, images):
    stacked = jnp.concatenate([table[:used, span] for table in tables], axis=0)
    found = [
        lax.dot_general(
            stacked, image[:, : span.stop - span.start], CONTRACT_LAST, preferred_element_type=F32
        )
        for image in images
    ]
    return jnp.concatenate(found, axis=1) if len(found) > 1 else found[0]


def first_kernel(count, used, *refs):
    *inputs, out = refs
    tables, images = inputs[:count], inputs[count:]
    out[...] = against(tables, used, slice(0, images[0].shape[1]), images)


def last_kernel(dims, *refs):
    n_img, known, steps, shifts, tiles, sig, n = dims
    count = len(steps)
    refs = list(refs)
    z, d = lax.axis_index("orient"), lax.axis_index("dom")
    firsts = [refs.pop(0) for _ in range(n_img - 1)]
    rests = [refs.pop(0) for _ in range(n_img)]
    tables = [refs.pop(0) for _ in range(count)]
    products = [refs.pop(0) for _ in range(count)]
    early = refs.pop(0) if known else None
    outs = refs
    pixels = tiles * LANES
    rows = rests[0].shape[0]
    codes = (products[0].shape[1] - rows) // 2
    total_rows = n_img * rows
    used = shifts * n
    cut = firsts[0].shape[1]
    beyond = pixels - cut

    crossed = against(tables, used, slice(cut, pixels), rests[1:])
    starts = [early[...]] if known else []
    if known < count:
        starts.append(against(tables[known:], used, slice(0, cut), firsts))
    crossed = crossed + (jnp.concatenate(starts, axis=0) if len(starts) > 1 else starts[0])
    extra = jnp.concatenate([rest[:, beyond:] for rest in rests], axis=0)
    take = (iota((16, LANES), 0) == iota((16, LANES), 1)).astype(BF16)
    turned = lax.dot_general(take, extra, CONTRACT_LAST, preferred_element_type=F32)
    beta = turned[1:2]
    power = turned[2 + sig : 3 + sig] + turned[3 + sig : 4 + sig] + turned[4 + sig : 5 + sig]
    power = power + pltpu.roll(power, total_rows - 1, 1)
    column = iota((total_rows, 6 * codes), 1)
    pick = (extra[:, 0:1].astype(F32).astype(jnp.int32) == column % codes).astype(BF16)
    squares = jnp.concatenate(
        [product[shifts * n : (shifts + 2) * n, rows:] for product in products], axis=0
    )
    terms = []
    for _ in range(3):
        term = squares.astype(BF16)
        terms.append(term)
        squares = squares - term.astype(F32)
    energies = lax.dot_general(
        jnp.concatenate(terms, axis=1), pick, CONTRACT_LAST, preferred_element_type=F32
    )

    even_row = iota((n, total_rows), 0) % 2 == 0
    same = (iota((n, total_rows), 0) % 2) == (iota((n, total_rows), 1) % 2)
    evidence = jnp.zeros((n, total_rows), F32)
    for c in range(count):
        energy = energies[2 * c * n : (2 * c + 1) * n] + energies[(2 * c + 1) * n : (2 * c + 2) * n]
        energy = energy + pltpu.roll(energy, n - 1, 0)
        scale = beta / jnp.sqrt(power * energy + EPSILON)
        cross = jnp.concatenate(
            [products[c][:used, :rows], crossed[c * used : (c + 1) * used]], axis=1
        )
        total = jnp.zeros((n, total_rows), F32)
        for t in range(shifts):
            value = jnp.where(same, cross[t * n : (t + 1) * n], 0.0)
            value = value + pltpu.roll(value, n - 1, 0)
            value = value + pltpu.roll(value, total_rows - 1, 1)
            total = total + jnp.exp(jnp.where(same & even_row, value * scale, 0.0))
        gid = (z ^ jnp.where(d == 0, *steps[c])).astype(F32)
        named = turned[2:3] == gid
        for s in range(1, sig):
            named = named | (turned[2 + s : 3 + s] == gid)
        evidence = evidence + jnp.where(even_row & named, total, 0.0)
    evidence = jnp.sum(evidence, axis=0, keepdims=True)
    spread = jnp.concatenate(
        [evidence, jnp.zeros((1, LANES - total_rows % LANES), F32)], axis=1
    ) if total_rows % LANES else evidence
    for i in range(n_img):
        here = spread if i == 0 else pltpu.roll(spread, LANES - i * rows, 1)
        outs[i][...] = jnp.where(iota((1, LANES), 1) < rows, here, 1.0)


def finish_kernel(rows, *refs):
    n_cls = len(refs) - 2
    post, log_out = refs[-2:]
    x = lax.axis_index("cls")
    place = iota((1, LANES), 1)
    used = (place % 2 == 0) & (place < 2 * rows)
    found = [jnp.where(used, r[...], 1.0) for r in refs[:n_cls]]
    total = found[0]
    for value in found[1:]:
        total = total + value
    row = iota((n_cls, LANES), 0)
    table = jnp.zeros((n_cls, LANES), F32)
    for k in range(n_cls):
        table = jnp.where(row == (x ^ k), found[k], table)
    squeeze = (iota((LANES, rows), 0) == 2 * iota((LANES, rows), 1)).astype(F32)
    both = jnp.concatenate([table / total, jnp.log(total)], axis=0)
    both = jnp.dot(both, squeeze, precision=lax.Precision.HIGHEST, preferred_element_type=F32)
    post[...] = both[:n_cls]
    log_out[...] = both[n_cls:]


def local(particles, ctf_index, beta, significant, ctf_table, references, offsets):
    groups = lax.axis_size("orient")
    n_cls = lax.axis_size("cls")
    cores = lax.axis_size("dom")
    blocks, sig = significant.shape
    rows, _, pixels = particles.shape
    per_block = rows // blocks
    codes = ctf_table.shape[0]
    oris = references.shape[2]
    shifts = offsets.shape[0]
    tiles = pixels // LANES
    refs_own = references.reshape(oris, 2, pixels)
    steps = list(range(1, groups))
    anywhere = pl.BlockSpec(memory_space=pl.ANY)
    vmem = pl.BlockSpec(memory_space=pltpu.VMEM)
    hbm = pl.BlockSpec(memory_space=pltpu.HBM)
    dma = pltpu.SemaphoreType.DMA

    def in_hbm(values):
        return pltpu.with_memory_space_constraint(values, pltpu.HBM)

    def core_step(first, second):
        pairs = []
        for a in range(groups):
            for core in range(cores):
                step = second if core else first
                pairs.append((a * cores + core, (a ^ step) * cores + core))
        return pairs

    swap = [(c, cores - 1 - c) for c in range(cores)]
    direct, order = [], []
    while len(steps) > 1:
        first, second = steps.pop(0), steps.pop(0)
        direct.append(
            lax.ppermute(refs_own, ("orient", "dom"), core_step(first, second))
        )
        order.append((first, second))
    last = steps.pop(0)

    def across(values, k):
        return lax.ppermute(values, "cls", [(c, c ^ k) for c in range(n_cls)])

    half = oris // 2
    cut = (tiles + 1) // 2 * LANES
    first_half, rest_half, part, ctf_near = pl.pallas_call(
        functools.partial(weigh_kernel, (rows, per_block, codes, sig)),
        name="weigh",
        out_shape=[
            jax.ShapeDtypeStruct((2 * rows, cut), BF16),
            jax.ShapeDtypeStruct((2 * rows, pixels - cut + LANES), BF16),
            jax.ShapeDtypeStruct((half, 2, pixels), BF16),
            jax.ShapeDtypeStruct((codes, pixels), BF16),
        ],
        in_specs=[hbm, hbm, hbm, hbm, hbm, hbm],
        out_specs=[vmem] * 4,
        scratch_shapes=[
            pltpu.SMEM((rows,), jnp.int32),
            pltpu.VMEM((1, rows), BF16),
            pltpu.SMEM((sig, blocks), jnp.int32),
            pltpu.VMEM((2 * rows, pixels), BF16),
            dma((2,)),
            dma((2,)),
            dma,
            dma((3,)),
        ],
        compiler_params=pltpu.CompilerParams(vmem_limit_bytes=16 << 20),
    )(
        in_hbm(ctf_index),
        in_hbm(beta[None]),
        in_hbm(significant.T),
        in_hbm(particles),
        in_hbm(ctf_table),
        in_hbm(refs_own),
    )
    firsts, rests = [], [rest_half]
    for k in range(1, n_cls):
        firsts.append(across(first_half, k))
        rests.append(across(rest_half, k))
    near_half = lax.ppermute(part, "orient", [(a, a ^ last) for a in range(groups)])
    lhs_rows = 2 * rows + 2 * codes
    phase_shape = jax.ShapeDtypeStruct((up(shifts, 8), pixels), F32)
    n = 2 * oris
    n_img = n_cls

    used = (shifts + 2) * n
    lhs, cosines, sines, *own = pl.pallas_call(
        functools.partial(prepare_kernel, tiles),
        name="prepare",
        out_shape=[
            jax.ShapeDtypeStruct((lhs_rows, pixels), BF16),
            phase_shape,
            phase_shape,
            jax.ShapeDtypeStruct((used, pixels), BF16),
            jax.ShapeDtypeStruct((used, lhs_rows), F32),
        ],
        in_specs=[vmem, vmem, vmem, hbm, hbm],
        out_specs=[vmem] * 5,
        scratch_shapes=[
            pltpu.VMEM((n, pixels), BF16),
            pltpu.SMEM((2, shifts), jnp.int32),
            dma,
            dma,
        ],
        compiler_params=pltpu.CompilerParams(vmem_limit_bytes=16 << 20),
    )(first_half, rest_half, ctf_near, in_hbm(offsets.T), in_hbm(refs_own))

    def make_table(*pieces):
        return pl.pallas_call(
            functools.partial(tables_kernel, shifts, tiles),
            name="tables",
            out_shape=[
                jax.ShapeDtypeStruct((used, pixels), BF16),
                jax.ShapeDtypeStruct((used, lhs_rows), F32),
            ],
            in_specs=[vmem, vmem, vmem] + [anywhere] * len(pieces),
            out_specs=[vmem, vmem],
            scratch_shapes=[pltpu.VMEM((n, pixels), BF16), dma],
            compiler_params=pltpu.CompilerParams(vmem_limit_bytes=12 << 20),
        )(lhs, cosines, sines, *pieces)

    def evaluate(group, early=()):
        steps, tables, products = zip(*group)
        known = early[0].shape[0] // (shifts * n) if early else 0
        return pl.pallas_call(
            functools.partial(last_kernel, (n_img, known, steps, shifts, tiles, sig, n)),
            name="last",
            out_shape=[jax.ShapeDtypeStruct((1, LANES), F32)] * n_img,
            in_specs=[vmem] * (2 * n_img - 1 + 2 * len(group) + len(early)),
            out_specs=[vmem] * n_img,
            compiler_params=pltpu.CompilerParams(
                vmem_limit_bytes=(12 << 20) if n_img < 4 else (40 << 20)
            ),
        )(*firsts, *rests, *tables, *products, *early)

    made = [((0, 0), *own)]
    for (first, second), near in zip(order, direct):
        mate = lax.ppermute(near, "dom", swap)
        made.append(((first, second), *make_table(near)))
        made.append(((second, first), *make_table(mate)))
    far_half = lax.ppermute(near_half, "dom", swap)
    made.append(((last, last), *make_table(near_half, far_half)))
    found = []
    while len(made) > SET:
        found.append(evaluate(made[:SET]))
        made = made[SET:]
    ready = [table for _, table, _ in made[:-1]]
    early = pl.pallas_call(
        functools.partial(first_kernel, len(ready), shifts * n),
        name="first",
        out_shape=jax.ShapeDtypeStruct(
            (len(ready) * shifts * n, (n_img - 1) * 2 * rows), F32
        ),
        in_specs=[vmem] * (len(ready) + n_img - 1),
        out_specs=vmem,
        compiler_params=pltpu.CompilerParams(
            vmem_limit_bytes=(12 << 20) if n_img < 4 else (40 << 20)
        ),
    )(*ready, *firsts)
    found.append(evaluate(made, (early,)))
    evidence = found[0]
    for more in found[1:]:
        evidence = [a + b for a, b in zip(evidence, more)]
    gathered = [evidence[0]] + [across(evidence[k], k) for k in range(1, n_cls)]
    post, log_total = pl.pallas_call(
        functools.partial(finish_kernel, rows),
        name="finish",
        out_shape=[
            jax.ShapeDtypeStruct((n_cls, rows), F32),
            jax.ShapeDtypeStruct((1, rows), F32),
        ],
        in_specs=[vmem] * n_cls,
        out_specs=[vmem, vmem],
        compiler_params=pltpu.CompilerParams(vmem_limit_bytes=8 << 20),
    )(*gathered)
    return (post.T, log_total.reshape(rows))


def solution(mesh):
    placed = (
        P(("groups", "orient", "cls", "dom"), None, None),
        P(("groups", "orient", "cls", "dom")),
        P(("groups", "orient", "cls", "dom")),
        P(("groups", "orient", "cls", "dom"), None),
        P(),
        P(("groups", "cls"), "orient", None, None, None),
        P("groups", None),
    )

    return jax.shard_map(
        local,
        mesh=mesh,
        in_specs=placed,
        out_specs=(
            P(("groups", "orient", "cls", "dom"), None),
            P(("groups", "orient", "cls", "dom")),
        ),
        check_vma=False,
    )
```

```python
import functools
import math

import jax
import jax.numpy as jnp
from jax import lax
from jax.experimental import pallas as pl
from jax.experimental.pallas import tpu as pltpu
from jax.sharding import PartitionSpec as P


BOX = 256
KX = 129
KY = 128

EPSILON = 1e-06
LANES = 128
UNROLL = 43
SET = 4
F32 = jnp.float32
BF16 = jnp.bfloat16
CONTRACT_LAST = (((1,), (1,)), ((), ()))


def lane(k, width=1, count=None):
    return pl.ds(pl.multiple_of(k * width * LANES, LANES), (count or width) * LANES)


def iota(shape, axis):
    return lax.broadcasted_iota(jnp.int32, shape, axis)


def weighted(pick, ctf, raw, span):
    value = raw[:, span].astype(F32)
    chosen = jnp.dot(pick, ctf[:, span], preferred_element_type=F32)
    return (chosen * value).astype(BF16), jnp.sum(value * value, axis=1, keepdims=True)


def picked(code, n_codes):
    shape = (code.shape[0], n_codes)
    return (code[:, 0:1] == iota(shape, 1)).astype(BF16)


def weigh_kernel(dims, codes_in, beta_in, groups_in, offsets_in, particles, ctf_in, refs,
                 first, raw, ctf, more, part, turns,
                 codes, beta, groups, offsets, sem, ctf_sem, half_sem, small_sem):
    rows, per_block, n_codes, sig = dims
    half = part.shape[0]
    small = [
        pltpu.make_async_copy(codes_in, codes, small_sem.at[0]),
        pltpu.make_async_copy(groups_in, groups, small_sem.at[1]),
        pltpu.make_async_copy(beta_in, beta, small_sem.at[2]),
        pltpu.make_async_copy(offsets_in, offsets, small_sem.at[3]),
    ]
    for copy in small:
        copy.start()
    cut, pixels = first.shape[1], raw.shape[1]
    spans = (slice(0, cut), slice(cut, pixels))
    loads = []
    for b, span in enumerate(spans):
        copies = [pltpu.make_async_copy(ctf_in.at[:, span], ctf.at[:, span], ctf_sem.at[b])]
        for p in range(rows):
            copies.append(
                pltpu.make_async_copy(
                    particles.at[p, :, span], raw.at[2 * p : 2 * p + 2, span], sem.at[b]
                )
            )
        loads.append(copies)
        for copy in copies:
            copy.start()
    half_copy = pltpu.make_async_copy(
        refs.at[pl.ds(lax.axis_index("dom") * half, half)], part, half_sem
    )
    half_copy.start()
    shape = (2 * rows, LANES)
    owner = iota(shape, 0) // 2
    column = iota(shape, 1)
    for copy in small:
        copy.wait()
    noise = beta[...].astype(F32)
    noise = jnp.where(iota((2 * rows, rows), 0) // 2 == iota((2 * rows, rows), 1), noise, 0.0)
    extra = jnp.where(column == 1, jnp.sum(noise, axis=1, keepdims=True), 0.0)
    code = jnp.zeros(shape, jnp.int32)
    for p in range(rows):
        mine = owner == p
        code = jnp.where(mine, codes[p], code)
        for s in range(sig):
            group = groups[s, p // per_block].astype(F32)
            extra = jnp.where(mine & (column == 2 + s), group, extra)
    extra = jnp.where(column == 0, code.astype(F32), extra)
    pick = picked(code, n_codes)
    for copy in loads[0]:
        copy.wait()
    first[...], power = weighted(pick, ctf, raw, spans[0])
    more[...] = jnp.where(column == 2 + sig, power, extra)
    shape = turns.shape[1:]
    step_x = jnp.zeros(shape, jnp.int32)
    step_y = jnp.zeros(shape, jnp.int32)
    for t in range(offsets.shape[1]):
        step_x = jnp.where(iota(shape, 0) == t, offsets[0, t], step_x)
        step_y = jnp.where(iota(shape, 0) == t, offsets[1, t], step_y)
    turns[0] = step_x * iota(shape, 1) - step_y * (KY // 2)
    turns[1] = step_y - step_x
    turns[2] = step_x * KX - step_y
    half_copy.wait()
    for copy in loads[1]:
        copy.wait()


def rest_kernel(sig, raw, ctf, more, rest):
    pixels, cut = raw.shape[1], raw.shape[1] + LANES - rest.shape[1]
    extra = more[...]
    column = iota(extra.shape, 1)
    pick = picked(extra.astype(jnp.int32), ctf.shape[0])
    rest[:, : pixels - cut], power = weighted(pick, ctf, raw, slice(cut, pixels))
    power = power + extra[:, 2 + sig : 3 + sig]
    for s in range(3):
        term = power.astype(BF16).astype(F32)
        extra = jnp.where(column == 2 + sig + s, term, extra)
        power = power - term
    rest[:, pixels - cut :] = extra.astype(BF16)


def up(value, to):
    return -(-value // to) * to


def block_copies(sources, raw, sem, b, width):
    span = lane(b * width, 1, width)
    copies, row = [], 0
    for source in sources:
        for i in range(source.shape[0]):
            copies.append(
                pltpu.make_async_copy(
                    source.at[i, :, span], raw.at[row : row + 2, span], sem.at[b]
                )
            )
            row += 2
    return copies


def load_blocks(sources, raw, sem):
    count = sem.shape[0]
    for b in range(count):
        for copy in block_copies(sources, raw, sem, b, raw.shape[1] // LANES // count):
            copy.start()


def build_table(sources, raw, sem, cosines, sines, lhs, table, product, shifts):
    n = raw.shape[0]
    odd = iota((n, LANES), 0) % 2 == 1
    count = sem.shape[0]
    width = raw.shape[1] // LANES // count

    def block(b, carry):
        for copy in block_copies(sources, raw, sem, b, width):
            copy.wait()

        def step(k, carry):
            here = lane(b * width + k)
            value = raw[:, here].astype(F32)
            turned = jnp.where(odd, -pltpu.roll(value, 1, 0), pltpu.roll(value, n - 1, 0))
            parts = [
                value * cosines[t : t + 1, here] + turned * sines[t : t + 1, here]
                for t in range(shifts)
            ]
            square = value * value
            high = square.astype(BF16).astype(F32)
            parts += [high, square - high]
            for i in range(0, len(parts), 2):
                both = jnp.concatenate(parts[i : i + 2], axis=0)
                table[n * i : n * i + both.shape[0], here] = both.astype(BF16)
            return carry

        return lax.fori_loop(0, width, step, carry, unroll=min(UNROLL, width))

    lax.fori_loop(0, count, block, 0)
    product[...] = lax.dot_general(
        table[...], lhs[...], CONTRACT_LAST, preferred_element_type=F32
    )


def prepare_kernel(shifts, first, rest, ctf, turns, refs, lhs, cosines, sines, table, product, raw, sem):
    load_blocks([refs], raw, sem)
    rows, codes = first.shape[0], ctf.shape[0]
    cut = first.shape[1]
    lhs[:rows, :cut] = first[...]
    lhs[:rows, cut:] = rest[:, : lhs.shape[1] - cut]
    place = iota(turns.shape[1:], 1)
    base, slope, wrapped = turns[0], turns[1], turns[2]

    def step(k, carry):
        value = ctf[:, lane(k)].astype(F32)
        square = value * value
        high = square.astype(BF16)
        lhs[rows : rows + codes, lane(k)] = high
        lhs[rows + codes :, lane(k)] = (square - high.astype(F32)).astype(BF16)
        turn = (base + slope * k + jnp.where(place < k, wrapped, 0)) & (BOX - 1)
        quarter = (turn + BOX // 8) >> 6
        x = (turn - (quarter << 6)).astype(F32) * (2.0 * math.pi / BOX)
        x2 = x * x
        sin = x + x * x2 * (
            -1.6666654611e-1 + x2 * (8.3321608736e-3 + x2 * -1.9515295891e-4)
        )
        cos = (1.0 - 0.5 * x2) + x2 * x2 * (
            4.166664568298827e-2 + x2 * (-1.388731625493765e-3 + x2 * 2.443315711809948e-5)
        )
        swap = (quarter & 1) == 1
        near = jnp.where(swap, sin, cos)
        other = jnp.where(swap, cos, sin)
        cosines[:, lane(k)] = jnp.where(((quarter + 1) & 2) == 2, -near, near)
        sines[:, lane(k)] = jnp.where((quarter & 2) == 2, -other, other)
        return carry

    lax.fori_loop(0, lhs.shape[1] // LANES, step, 0, unroll=UNROLL)
    build_table([refs], raw, sem, cosines, sines, lhs, table, product, shifts)


def tables_kernel(shifts, lhs, cosines, sines, *refs):
    table, product, raw, sem = refs[-4:]
    load_blocks(refs[:-4], raw, sem)
    build_table(refs[:-4], raw, sem, cosines, sines, lhs, table, product, shifts)


def against(tables, used, span, images):
    stacked = jnp.concatenate([table[:used, span] for table in tables], axis=0)
    found = [
        lax.dot_general(
            stacked, image[:, : span.stop - span.start], CONTRACT_LAST, preferred_element_type=F32
        )
        for image in images
    ]
    return jnp.concatenate(found, axis=1) if len(found) > 1 else found[0]


def first_kernel(count, used, *refs):
    *inputs, out = refs
    tables, images = inputs[:count], inputs[count:]
    out[...] = against(tables, used, slice(0, images[0].shape[1]), images)


def last_kernel(dims, *refs):
    n_img, known, steps, shifts, tiles, sig, n = dims
    count = len(steps)
    refs = list(refs)
    z, d = lax.axis_index("orient"), lax.axis_index("dom")
    firsts = [refs.pop(0) for _ in range(n_img - 1)]
    rests = [refs.pop(0) for _ in range(n_img)]
    tables = [refs.pop(0) for _ in range(count)]
    products = [refs.pop(0) for _ in range(count)]
    early = refs.pop(0) if known else None
    outs = refs
    pixels = tiles * LANES
    rows = rests[0].shape[0]
    codes = (products[0].shape[1] - rows) // 2
    total_rows = n_img * rows
    used = shifts * n
    beyond = rests[0].shape[1] - LANES

    crossed = against(tables, used, slice(pixels - beyond, pixels), rests[1:])
    starts = [early[...]] if known else []
    if known < count:
        starts.append(against(tables[known:], used, slice(0, pixels - beyond), firsts))
    crossed = crossed + (jnp.concatenate(starts, axis=0) if len(starts) > 1 else starts[0])
    extra = jnp.concatenate([rest[:, beyond:] for rest in rests], axis=0)
    take = (iota((16, LANES), 0) == iota((16, LANES), 1)).astype(BF16)
    turned = lax.dot_general(take, extra, CONTRACT_LAST, preferred_element_type=F32)
    beta = turned[1:2]
    power = turned[2 + sig : 3 + sig] + turned[3 + sig : 4 + sig] + turned[4 + sig : 5 + sig]
    power = power + pltpu.roll(power, total_rows - 1, 1)
    column = iota((total_rows, 6 * codes), 1)
    pick = (extra[:, 0:1].astype(F32).astype(jnp.int32) == column % codes).astype(BF16)
    squares = jnp.concatenate(
        [product[shifts * n : (shifts + 2) * n, rows:] for product in products], axis=0
    )
    terms = []
    for _ in range(3):
        term = squares.astype(BF16)
        terms.append(term)
        squares = squares - term.astype(F32)
    energies = lax.dot_general(
        jnp.concatenate(terms, axis=1), pick, CONTRACT_LAST, preferred_element_type=F32
    )

    even_row = iota((n, total_rows), 0) % 2 == 0
    same = (iota((n, total_rows), 0) % 2) == (iota((n, total_rows), 1) % 2)
    evidence = jnp.zeros((n, total_rows), F32)
    for c in range(count):
        energy = energies[2 * c * n : (2 * c + 1) * n] + energies[(2 * c + 1) * n : (2 * c + 2) * n]
        energy = energy + pltpu.roll(energy, n - 1, 0)
        scale = beta / jnp.sqrt(power * energy + EPSILON)
        cross = jnp.concatenate(
            [products[c][:used, :rows], crossed[c * used : (c + 1) * used]], axis=1
        )
        total = jnp.zeros((n, total_rows), F32)
        for t in range(shifts):
            value = jnp.where(same, cross[t * n : (t + 1) * n], 0.0)
            value = value + pltpu.roll(value, n - 1, 0)
            value = value + pltpu.roll(value, total_rows - 1, 1)
            total = total + jnp.exp(jnp.where(same & even_row, value * scale, 0.0))
        gid = (z ^ jnp.where(d == 0, *steps[c])).astype(F32)
        named = turned[2:3] == gid
        for s in range(1, sig):
            named = named | (turned[2 + s : 3 + s] == gid)
        evidence = evidence + jnp.where(even_row & named, total, 0.0)
    evidence = jnp.sum(evidence, axis=0, keepdims=True)
    spread = jnp.concatenate(
        [evidence, jnp.zeros((1, LANES - total_rows % LANES), F32)], axis=1
    ) if total_rows % LANES else evidence
    for i in range(n_img):
        here = spread if i == 0 else pltpu.roll(spread, LANES - i * rows, 1)
        outs[i][...] = jnp.where(iota((1, LANES), 1) < rows, here, 1.0)


def finish_kernel(rows, *refs):
    n_cls = len(refs) - 2
    post, log_out = refs[-2:]
    x = lax.axis_index("cls")
    place = iota((1, LANES), 1)
    used = (place % 2 == 0) & (place < 2 * rows)
    found = [jnp.where(used, r[...], 1.0) for r in refs[:n_cls]]
    total = found[0]
    for value in found[1:]:
        total = total + value
    row = iota((n_cls, LANES), 0)
    table = jnp.zeros((n_cls, LANES), F32)
    for k in range(n_cls):
        table = jnp.where(row == (x ^ k), found[k], table)
    squeeze = (iota((LANES, rows), 0) == 2 * iota((LANES, rows), 1)).astype(F32)
    both = jnp.concatenate([table / total, jnp.log(total)], axis=0)
    both = jnp.dot(both, squeeze, precision=lax.Precision.HIGHEST, preferred_element_type=F32)
    post[...] = both[:n_cls]
    log_out[...] = both[n_cls:]


def local(particles, ctf_index, beta, significant, ctf_table, references, offsets):
    groups = lax.axis_size("orient")
    n_cls = lax.axis_size("cls")
    cores = lax.axis_size("dom")
    blocks_here, sig = significant.shape
    rows, _, pixels = particles.shape
    per_block = rows // blocks_here
    codes = ctf_table.shape[0]
    oris = references.shape[2]
    shifts = offsets.shape[0]
    tiles = pixels // LANES
    refs_own = references.reshape(oris, 2, pixels)
    steps = [k for k in range(1, groups) if k != groups // 2] + [groups // 2]
    anywhere = pl.BlockSpec(memory_space=pl.ANY)
    vmem = pl.BlockSpec(memory_space=pltpu.VMEM)
    hbm = pl.BlockSpec(memory_space=pltpu.HBM)
    dma = pltpu.SemaphoreType.DMA

    def in_hbm(values):
        return pltpu.with_memory_space_constraint(values, pltpu.HBM)

    def core_step(first, second):
        pairs = []
        for a in range(groups):
            for core in range(cores):
                step = second if core else first
                pairs.append((a * cores + core, (a ^ step) * cores + core))
        return pairs

    swap = [(c, cores - 1 - c) for c in range(cores)]
    direct, order = [], []
    while len(steps) > 1:
        low, high = steps.pop(0), steps.pop(0)
        direct.append(lax.ppermute(refs_own, ("orient", "dom"), core_step(low, high)))
        order.append((low, high))
    last = steps.pop(0)

    def across(values, k):
        return lax.ppermute(values, "cls", [(c, c ^ k) for c in range(n_cls)])

    half = oris // 2
    cut = tiles * 3 // 4 * LANES
    first, raw_rows, ctf_near, more, part, turns = pl.pallas_call(
        functools.partial(weigh_kernel, (rows, per_block, codes, sig)),
        name="weigh",
        out_shape=[
            jax.ShapeDtypeStruct((2 * rows, cut), BF16),
            jax.ShapeDtypeStruct((2 * rows, pixels), BF16),
            jax.ShapeDtypeStruct((codes, pixels), BF16),
            jax.ShapeDtypeStruct((2 * rows, LANES), F32),
            jax.ShapeDtypeStruct((half, 2, pixels), BF16),
            jax.ShapeDtypeStruct((3, up(shifts, 8), LANES), jnp.int32),
        ],
        in_specs=[hbm] * 7,
        out_specs=[vmem] * 6,
        scratch_shapes=[
            pltpu.SMEM((rows,), jnp.int32),
            pltpu.VMEM((1, rows), BF16),
            pltpu.SMEM((sig, blocks_here), jnp.int32),
            pltpu.SMEM((2, shifts), jnp.int32),
            dma((2,)),
            dma((2,)),
            dma,
            dma((4,)),
        ],
        compiler_params=pltpu.CompilerParams(vmem_limit_bytes=16 << 20),
    )(
        in_hbm(ctf_index),
        in_hbm(beta[None]),
        in_hbm(significant.T),
        in_hbm(offsets.T),
        in_hbm(particles),
        in_hbm(ctf_table),
        in_hbm(refs_own),
    )
    rest = pl.pallas_call(
        functools.partial(rest_kernel, sig),
        name="rest",
        out_shape=jax.ShapeDtypeStruct((2 * rows, pixels - cut + LANES), BF16),
        in_specs=[vmem] * 3,
        out_specs=vmem,
        compiler_params=pltpu.CompilerParams(vmem_limit_bytes=12 << 20),
    )(raw_rows, ctf_near, more)
    firsts, rests = [], [rest]
    for k in range(1, n_cls):
        firsts.append(across(first, k))
        rests.append(across(rest, k))
    near_half = lax.ppermute(part, "orient", [(a, a ^ last) for a in range(groups)])
    lhs_rows = 2 * rows + 2 * codes
    phase_shape = jax.ShapeDtypeStruct((up(shifts, 8), pixels), F32)
    n = 2 * oris
    n_img = n_cls
    n_blocks = 3 if tiles % 3 == 0 else 1

    used = (shifts + 2) * n
    lhs, cosines, sines, *own = pl.pallas_call(
        functools.partial(prepare_kernel, shifts),
        name="prepare",
        out_shape=[
            jax.ShapeDtypeStruct((lhs_rows, pixels), BF16),
            phase_shape,
            phase_shape,
            jax.ShapeDtypeStruct((used, pixels), BF16),
            jax.ShapeDtypeStruct((used, lhs_rows), F32),
        ],
        in_specs=[vmem] * 4 + [hbm],
        out_specs=[vmem] * 5,
        scratch_shapes=[pltpu.VMEM((n, pixels), BF16), dma((n_blocks,))],
        compiler_params=pltpu.CompilerParams(vmem_limit_bytes=16 << 20),
    )(first, rest, ctf_near, turns, in_hbm(refs_own))

    def make_table(*pieces):
        return pl.pallas_call(
            functools.partial(tables_kernel, shifts),
            name="tables",
            out_shape=[
                jax.ShapeDtypeStruct((used, pixels), BF16),
                jax.ShapeDtypeStruct((used, lhs_rows), F32),
            ],
            in_specs=[vmem, vmem, vmem] + [anywhere] * len(pieces),
            out_specs=[vmem, vmem],
            scratch_shapes=[pltpu.VMEM((n, pixels), BF16), dma((n_blocks,))],
            compiler_params=pltpu.CompilerParams(vmem_limit_bytes=12 << 20),
        )(lhs, cosines, sines, *pieces)

    def evaluate(group, early=()):
        steps, tables, products = zip(*group)
        known = early[0].shape[0] // (shifts * n) if early else 0
        return pl.pallas_call(
            functools.partial(last_kernel, (n_img, known, steps, shifts, tiles, sig, n)),
            name="last",
            out_shape=[jax.ShapeDtypeStruct((1, LANES), F32)] * n_img,
            in_specs=[vmem] * (2 * n_img - 1 + 2 * len(group) + len(early)),
            out_specs=[vmem] * n_img,
            compiler_params=pltpu.CompilerParams(
                vmem_limit_bytes=(12 << 20) if n_img < 4 else (40 << 20)
            ),
        )(*firsts, *rests, *tables, *products, *early)

    made = [((0, 0), *own)]
    for (low, high), near in zip(order, direct):
        mate = lax.ppermute(near, "dom", swap)
        made.append(((low, high), *make_table(near)))
        made.append(((high, low), *make_table(mate)))
    far_half = lax.ppermute(near_half, "dom", swap)
    made.append(((last, last), *make_table(near_half, far_half)))
    found = []
    while len(made) > SET:
        found.append(evaluate(made[:SET]))
        made = made[SET:]
    ready = [table for _, table, _ in made[:-1]]
    early = pl.pallas_call(
        functools.partial(first_kernel, len(ready), shifts * n),
        name="first",
        out_shape=jax.ShapeDtypeStruct(
            (len(ready) * shifts * n, (n_img - 1) * 2 * rows), F32
        ),
        in_specs=[vmem] * (len(ready) + n_img - 1),
        out_specs=vmem,
        compiler_params=pltpu.CompilerParams(
            vmem_limit_bytes=(12 << 20) if n_img < 4 else (40 << 20)
        ),
    )(*ready, *firsts)
    found.append(evaluate(made, (early,)))
    evidence = found[0]
    for more in found[1:]:
        evidence = [a + b for a, b in zip(evidence, more)]
    gathered = [evidence[0]] + [across(evidence[k], k) for k in range(1, n_cls)]
    post, log_total = pl.pallas_call(
        functools.partial(finish_kernel, rows),
        name="finish",
        out_shape=[
            jax.ShapeDtypeStruct((n_cls, rows), F32),
            jax.ShapeDtypeStruct((1, rows), F32),
        ],
        in_specs=[vmem] * n_cls,
        out_specs=[vmem, vmem],
        compiler_params=pltpu.CompilerParams(vmem_limit_bytes=8 << 20),
    )(*gathered)
    return (post.T, log_total.reshape(rows))


def solution(mesh):
    placed = (
        P(("groups", "orient", "cls", "dom"), None, None),
        P(("groups", "orient", "cls", "dom")),
        P(("groups", "orient", "cls", "dom")),
        P(("groups", "orient", "cls", "dom"), None),
        P(),
        P(("groups", "cls"), "orient", None, None, None),
        P("groups", None),
    )

    return jax.shard_map(
        local,
        mesh=mesh,
        in_specs=placed,
        out_specs=(
            P(("groups", "orient", "cls", "dom"), None),
            P(("groups", "orient", "cls", "dom")),
        ),
        check_vma=False,
    )
```

```python
import functools
import math

import jax
import jax.numpy as jnp
from jax import lax
from jax.experimental import pallas as pl
from jax.experimental.pallas import tpu as pltpu
from jax.sharding import PartitionSpec as P


BOX = 256
KX = 129
KY = 128

EPSILON = 1e-06
LANES = 128
UNROLL = 43
SET = 4
F32 = jnp.float32
BF16 = jnp.bfloat16
CONTRACT_LAST = (((1,), (1,)), ((), ()))


def lane(k, width=1, count=None):
    return pl.ds(pl.multiple_of(k * width * LANES, LANES), (count or width) * LANES)


def iota(shape, axis):
    return lax.broadcasted_iota(jnp.int32, shape, axis)


def weighted(pick, ctf, raw, span):
    value = raw[:, span].astype(F32)
    chosen = jnp.dot(pick, ctf[:, span], preferred_element_type=F32)
    return (chosen * value).astype(BF16), jnp.sum(value * value, axis=1, keepdims=True)


def picked(code, n_codes):
    shape = (code.shape[0], n_codes)
    return (code[:, 0:1] == iota(shape, 1)).astype(BF16)


def weigh_kernel(dims, codes_in, beta_in, groups_in, offsets_in, particles, ctf_in, refs,
                 first, raw, ctf, more, part, turns,
                 codes, beta, groups, offsets, sem, ctf_sem, half_sem, small_sem):
    rows, per_block, n_codes, sig = dims
    half = part.shape[0]
    small = [
        pltpu.make_async_copy(codes_in, codes, small_sem.at[0]),
        pltpu.make_async_copy(groups_in, groups, small_sem.at[1]),
        pltpu.make_async_copy(beta_in, beta, small_sem.at[2]),
        pltpu.make_async_copy(offsets_in, offsets, small_sem.at[3]),
    ]
    cut, pixels = first.shape[1], raw.shape[1]
    spans = (slice(0, cut), slice(cut, pixels))
    loads = []
    for b, span in enumerate(spans):
        copies = [pltpu.make_async_copy(ctf_in.at[:, span], ctf.at[:, span], ctf_sem.at[b])]
        for p in range(rows):
            copies.append(
                pltpu.make_async_copy(
                    particles.at[p, :, span], raw.at[2 * p : 2 * p + 2, span], sem.at[b]
                )
            )
        loads.append(copies)
        for copy in copies:
            copy.start()
        if b == 0:
            for copy in small:
                copy.start()
    half_copy = pltpu.make_async_copy(
        refs.at[pl.ds(lax.axis_index("dom") * half, half)], part, half_sem
    )
    half_copy.start()
    shape = (2 * rows, LANES)
    owner = iota(shape, 0) // 2
    column = iota(shape, 1)
    for copy in small:
        copy.wait()
    noise = beta[...].astype(F32)
    noise = jnp.where(iota((2 * rows, rows), 0) // 2 == iota((2 * rows, rows), 1), noise, 0.0)
    extra = jnp.where(column == 1, jnp.sum(noise, axis=1, keepdims=True), 0.0)
    code = jnp.zeros(shape, jnp.int32)
    for p in range(rows):
        mine = owner == p
        code = jnp.where(mine, codes[p], code)
        for s in range(sig):
            group = groups[s, p // per_block].astype(F32)
            extra = jnp.where(mine & (column == 2 + s), group, extra)
    extra = jnp.where(column == 0, code.astype(F32), extra)
    phases = turns.shape[1:]
    step_x = jnp.zeros(phases, jnp.int32)
    step_y = jnp.zeros(phases, jnp.int32)
    for t in range(offsets.shape[1]):
        step_x = jnp.where(iota(phases, 0) == t, offsets[0, t], step_x)
        step_y = jnp.where(iota(phases, 0) == t, offsets[1, t], step_y)
    turns[0] = step_x * iota(phases, 1) - step_y * (KY // 2)
    turns[1] = step_y - step_x
    turns[2] = step_x * KX - step_y
    pick = picked(code, n_codes)
    for copy in loads[0]:
        copy.wait()
    first[...], power = weighted(pick, ctf, raw, spans[0])
    more[...] = jnp.where(column == 2 + sig, power, extra)
    half_copy.wait()
    for copy in loads[1]:
        copy.wait()


def rest_kernel(sig, raw, ctf, more, rest):
    pixels, cut = raw.shape[1], raw.shape[1] + LANES - rest.shape[1]
    extra = more[...]
    column = iota(extra.shape, 1)
    pick = picked(extra.astype(jnp.int32), ctf.shape[0])
    rest[:, : pixels - cut], power = weighted(pick, ctf, raw, slice(cut, pixels))
    power = power + extra[:, 2 + sig : 3 + sig]
    for s in range(3):
        term = power.astype(BF16).astype(F32)
        extra = jnp.where(column == 2 + sig + s, term, extra)
        power = power - term
    rest[:, pixels - cut :] = extra.astype(BF16)


def up(value, to):
    return -(-value // to) * to


def block_copies(sources, raw, sem, b, width):
    span = lane(b * width, 1, width)
    copies, row = [], 0
    for source in sources:
        for i in range(source.shape[0]):
            copies.append(
                pltpu.make_async_copy(
                    source.at[i, :, span], raw.at[row : row + 2, span], sem.at[b]
                )
            )
            row += 2
    return copies


def load_blocks(sources, raw, sem):
    count = sem.shape[0]
    for b in range(count):
        for copy in block_copies(sources, raw, sem, b, raw.shape[1] // LANES // count):
            copy.start()


def build_table(sources, raw, sem, cosines, sines, lhs, table, product, shifts, images=(), cross=None):
    n = raw.shape[0]
    odd = iota((n, LANES), 0) % 2 == 1
    count = sem.shape[0]
    width = raw.shape[1] // LANES // count

    def block(b, carry):
        for copy in block_copies(sources, raw, sem, b, width):
            copy.wait()

        def step(k, carry):
            here = lane(b * width + k)
            value = raw[:, here].astype(F32)
            turned = jnp.where(odd, -pltpu.roll(value, 1, 0), pltpu.roll(value, n - 1, 0))
            parts = [
                value * cosines[t : t + 1, here] + turned * sines[t : t + 1, here]
                for t in range(shifts)
            ]
            square = value * value
            high = square.astype(BF16).astype(F32)
            parts += [high, square - high]
            for i in range(0, len(parts), 2):
                both = jnp.concatenate(parts[i : i + 2], axis=0)
                table[n * i : n * i + both.shape[0], here] = both.astype(BF16)
            return carry

        return lax.fori_loop(0, width, step, carry, unroll=min(UNROLL, width))

    lax.fori_loop(0, count, block, 0)
    if not images:
        product[...] = lax.dot_general(
            table[...], lhs[...], CONTRACT_LAST, preferred_element_type=F32
        )
        return
    cut, width = images[0].shape[1], lhs.shape[0]
    right = jnp.concatenate([lhs[:, :cut]] + [image[...] for image in images], axis=0)
    both = lax.dot_general(
        table[:, :cut], right, CONTRACT_LAST, preferred_element_type=F32
    )
    product[...] = both[:, :width] + lax.dot_general(
        table[:, cut:], lhs[:, cut:], CONTRACT_LAST, preferred_element_type=F32
    )
    cross[...] = both[: cross.shape[0], width:]


def prepare_kernel(shifts, first, rest, ctf, turns, refs, lhs, cosines, sines, table, product, raw, sem):
    load_blocks([refs], raw, sem)
    rows, codes = first.shape[0], ctf.shape[0]
    cut = first.shape[1]
    lhs[:rows, :cut] = first[...]
    lhs[:rows, cut:] = rest[:, : lhs.shape[1] - cut]
    place = iota(turns.shape[1:], 1)
    base, slope, wrapped = turns[0], turns[1], turns[2]

    def step(k, carry):
        value = ctf[:, lane(k)].astype(F32)
        square = value * value
        high = square.astype(BF16)
        lhs[rows : rows + codes, lane(k)] = high
        lhs[rows + codes :, lane(k)] = (square - high.astype(F32)).astype(BF16)
        turn = (base + slope * k + jnp.where(place < k, wrapped, 0)) & (BOX - 1)
        quarter = (turn + BOX // 8) >> 6
        x = (turn - (quarter << 6)).astype(F32) * (2.0 * math.pi / BOX)
        x2 = x * x
        sin = x + x * x2 * (
            -1.6666654611e-1 + x2 * (8.3321608736e-3 + x2 * -1.9515295891e-4)
        )
        cos = (1.0 - 0.5 * x2) + x2 * x2 * (
            4.166664568298827e-2 + x2 * (-1.388731625493765e-3 + x2 * 2.443315711809948e-5)
        )
        swap = (quarter & 1) == 1
        near = jnp.where(swap, sin, cos)
        other = jnp.where(swap, cos, sin)
        cosines[:, lane(k)] = jnp.where(((quarter + 1) & 2) == 2, -near, near)
        sines[:, lane(k)] = jnp.where((quarter & 2) == 2, -other, other)
        return carry

    lax.fori_loop(0, lhs.shape[1] // LANES, step, 0, unroll=UNROLL)
    build_table([refs], raw, sem, cosines, sines, lhs, table, product, shifts)


def tables_kernel(shifts, n_other, lhs, cosines, sines, *refs):
    images, refs = refs[:n_other], refs[n_other:]
    raw, sem = refs[-2:]
    n_out = 3 if images else 2
    pieces, outs = refs[: -2 - n_out], refs[-2 - n_out : -2]
    load_blocks(pieces, raw, sem)
    build_table(pieces, raw, sem, cosines, sines, lhs, outs[0], outs[1], shifts, images, outs[-1])


def against(tables, used, span, images):
    stacked = jnp.concatenate([table[:used, span] for table in tables], axis=0)
    found = [
        lax.dot_general(
            stacked, image[:, : span.stop - span.start], CONTRACT_LAST, preferred_element_type=F32
        )
        for image in images
    ]
    return jnp.concatenate(found, axis=1) if len(found) > 1 else found[0]


def first_kernel(count, used, *refs):
    *inputs, out = refs
    tables, images = inputs[:count], inputs[count:]
    out[...] = against(tables, used, slice(0, images[0].shape[1]), images)


def last_kernel(dims, *refs):
    n_img, n_early, steps, shifts, tiles, sig, n = dims
    count = len(steps)
    refs = list(refs)
    z, d = lax.axis_index("orient"), lax.axis_index("dom")
    firsts = [refs.pop(0) for _ in range(n_img - 1)]
    rests = [refs.pop(0) for _ in range(n_img)]
    tables = [refs.pop(0) for _ in range(count)]
    products = [refs.pop(0) for _ in range(count)]
    starts = [refs.pop(0)[...] for _ in range(n_early)]
    outs = refs
    pixels = tiles * LANES
    rows = rests[0].shape[0]
    codes = (products[0].shape[1] - rows) // 2
    total_rows = n_img * rows
    used = shifts * n
    beyond = rests[0].shape[1] - LANES

    crossed = against(tables, used, slice(pixels - beyond, pixels), rests[1:])
    if not starts:
        starts = [against(tables, used, slice(0, pixels - beyond), firsts)]
    crossed = crossed + (jnp.concatenate(starts, axis=0) if len(starts) > 1 else starts[0])
    extra = jnp.concatenate([rest[:, beyond:] for rest in rests], axis=0)
    take = (iota((16, LANES), 0) == iota((16, LANES), 1)).astype(BF16)
    turned = lax.dot_general(take, extra, CONTRACT_LAST, preferred_element_type=F32)
    beta = turned[1:2]
    power = turned[2 + sig : 3 + sig] + turned[3 + sig : 4 + sig] + turned[4 + sig : 5 + sig]
    power = power + pltpu.roll(power, total_rows - 1, 1)
    column = iota((total_rows, 6 * codes), 1)
    pick = (extra[:, 0:1].astype(F32).astype(jnp.int32) == column % codes).astype(BF16)
    squares = jnp.concatenate(
        [product[shifts * n : (shifts + 2) * n, rows:] for product in products], axis=0
    )
    terms = []
    for _ in range(3):
        term = squares.astype(BF16)
        terms.append(term)
        squares = squares - term.astype(F32)
    energies = lax.dot_general(
        jnp.concatenate(terms, axis=1), pick, CONTRACT_LAST, preferred_element_type=F32
    )

    even_row = iota((n, total_rows), 0) % 2 == 0
    same = (iota((n, total_rows), 0) % 2) == (iota((n, total_rows), 1) % 2)
    evidence = jnp.zeros((n, total_rows), F32)
    for c in range(count):
        energy = energies[2 * c * n : (2 * c + 1) * n] + energies[(2 * c + 1) * n : (2 * c + 2) * n]
        energy = energy + pltpu.roll(energy, n - 1, 0)
        scale = beta / jnp.sqrt(power * energy + EPSILON)
        cross = jnp.concatenate(
            [products[c][:used, :rows], crossed[c * used : (c + 1) * used]], axis=1
        )
        total = jnp.zeros((n, total_rows), F32)
        for t in range(shifts):
            value = jnp.where(same, cross[t * n : (t + 1) * n], 0.0)
            value = value + pltpu.roll(value, n - 1, 0)
            value = value + pltpu.roll(value, total_rows - 1, 1)
            total = total + jnp.exp(jnp.where(same & even_row, value * scale, 0.0))
        gid = (z ^ jnp.where(d == 0, *steps[c])).astype(F32)
        named = turned[2:3] == gid
        for s in range(1, sig):
            named = named | (turned[2 + s : 3 + s] == gid)
        evidence = evidence + jnp.where(even_row & named, total, 0.0)
    evidence = jnp.sum(evidence, axis=0, keepdims=True)
    spread = jnp.concatenate(
        [evidence, jnp.zeros((1, LANES - total_rows % LANES), F32)], axis=1
    ) if total_rows % LANES else evidence
    for i in range(n_img):
        here = spread if i == 0 else pltpu.roll(spread, LANES - i * rows, 1)
        outs[i][...] = jnp.where(iota((1, LANES), 1) < rows, here, 1.0)


def finish_kernel(rows, *refs):
    n_cls = len(refs) - 2
    post, log_out = refs[-2:]
    x = lax.axis_index("cls")
    place = iota((1, LANES), 1)
    used = (place % 2 == 0) & (place < 2 * rows)
    found = [jnp.where(used, r[...], 1.0) for r in refs[:n_cls]]
    total = found[0]
    for value in found[1:]:
        total = total + value
    row = iota((n_cls, LANES), 0)
    table = jnp.zeros((n_cls, LANES), F32)
    for k in range(n_cls):
        table = jnp.where(row == (x ^ k), found[k], table)
    squeeze = (iota((LANES, rows), 0) == 2 * iota((LANES, rows), 1)).astype(F32)
    both = jnp.concatenate([table / total, jnp.log(total)], axis=0)
    both = jnp.dot(both, squeeze, precision=lax.Precision.HIGHEST, preferred_element_type=F32)
    post[...] = both[:n_cls]
    log_out[...] = both[n_cls:]


def local(particles, ctf_index, beta, significant, ctf_table, references, offsets):
    groups = lax.axis_size("orient")
    n_cls = lax.axis_size("cls")
    cores = lax.axis_size("dom")
    blocks_here, sig = significant.shape
    rows, _, pixels = particles.shape
    per_block = rows // blocks_here
    codes = ctf_table.shape[0]
    oris = references.shape[2]
    shifts = offsets.shape[0]
    tiles = pixels // LANES
    refs_own = references.reshape(oris, 2, pixels)
    steps = [k for k in range(1, groups) if k != groups // 2] + [groups // 2]
    anywhere = pl.BlockSpec(memory_space=pl.ANY)
    vmem = pl.BlockSpec(memory_space=pltpu.VMEM)
    hbm = pl.BlockSpec(memory_space=pltpu.HBM)
    dma = pltpu.SemaphoreType.DMA

    def in_hbm(values):
        return pltpu.with_memory_space_constraint(values, pltpu.HBM)

    def core_step(first, second):
        pairs = []
        for a in range(groups):
            for core in range(cores):
                step = second if core else first
                pairs.append((a * cores + core, (a ^ step) * cores + core))
        return pairs

    swap = [(c, cores - 1 - c) for c in range(cores)]
    direct, order = [], []
    while len(steps) > 1:
        low, high = steps.pop(0), steps.pop(0)
        direct.append(lax.ppermute(refs_own, ("orient", "dom"), core_step(low, high)))
        order.append((low, high))
    last = steps.pop(0)

    def across(values, k):
        return lax.ppermute(values, "cls", [(c, c ^ k) for c in range(n_cls)])

    half = oris // 2
    cut = tiles * 3 // 4 * LANES
    first, raw_rows, ctf_near, more, part, turns = pl.pallas_call(
        functools.partial(weigh_kernel, (rows, per_block, codes, sig)),
        name="weigh",
        out_shape=[
            jax.ShapeDtypeStruct((2 * rows, cut), BF16),
            jax.ShapeDtypeStruct((2 * rows, pixels), BF16),
            jax.ShapeDtypeStruct((codes, pixels), BF16),
            jax.ShapeDtypeStruct((2 * rows, LANES), F32),
            jax.ShapeDtypeStruct((half, 2, pixels), BF16),
            jax.ShapeDtypeStruct((3, up(shifts, 8), LANES), jnp.int32),
        ],
        in_specs=[hbm] * 7,
        out_specs=[vmem] * 6,
        scratch_shapes=[
            pltpu.SMEM((rows,), jnp.int32),
            pltpu.VMEM((1, rows), BF16),
            pltpu.SMEM((sig, blocks_here), jnp.int32),
            pltpu.SMEM((2, shifts), jnp.int32),
            dma((2,)),
            dma((2,)),
            dma,
            dma((4,)),
        ],
        compiler_params=pltpu.CompilerParams(vmem_limit_bytes=16 << 20),
    )(
        in_hbm(ctf_index),
        in_hbm(beta[None]),
        in_hbm(significant.T),
        in_hbm(offsets.T),
        in_hbm(particles),
        in_hbm(ctf_table),
        in_hbm(refs_own),
    )
    rest = pl.pallas_call(
        functools.partial(rest_kernel, sig),
        name="rest",
        out_shape=jax.ShapeDtypeStruct((2 * rows, pixels - cut + LANES), BF16),
        in_specs=[vmem] * 3,
        out_specs=vmem,
        compiler_params=pltpu.CompilerParams(vmem_limit_bytes=12 << 20),
    )(raw_rows, ctf_near, more)
    firsts, rests = [], [rest]
    for k in range(1, n_cls):
        firsts.append(across(first, k))
        rests.append(across(rest, k))
    near_half = lax.ppermute(part, "orient", [(a, a ^ last) for a in range(groups)])
    lhs_rows = 2 * rows + 2 * codes
    phase_shape = jax.ShapeDtypeStruct((up(shifts, 8), pixels), F32)
    n = 2 * oris
    n_img = n_cls
    n_blocks = 3 if tiles % 3 == 0 else 1

    used = (shifts + 2) * n
    lhs, cosines, sines, *own = pl.pallas_call(
        functools.partial(prepare_kernel, shifts),
        name="prepare",
        out_shape=[
            jax.ShapeDtypeStruct((lhs_rows, pixels), BF16),
            phase_shape,
            phase_shape,
            jax.ShapeDtypeStruct((used, pixels), BF16),
            jax.ShapeDtypeStruct((used, lhs_rows), F32),
        ],
        in_specs=[vmem] * 4 + [hbm],
        out_specs=[vmem] * 5,
        scratch_shapes=[pltpu.VMEM((n, pixels), BF16), dma((n_blocks,))],
        compiler_params=pltpu.CompilerParams(vmem_limit_bytes=16 << 20),
    )(first, rest, ctf_near, turns, in_hbm(refs_own))

    def make_table(*pieces, images=()):
        outs = [
            jax.ShapeDtypeStruct((used, pixels), BF16),
            jax.ShapeDtypeStruct((used, lhs_rows), F32),
        ]
        if images:
            outs.append(
                jax.ShapeDtypeStruct((shifts * n, len(images) * 2 * rows), F32)
            )
        return pl.pallas_call(
            functools.partial(tables_kernel, shifts, len(images)),
            name="tables",
            out_shape=outs,
            in_specs=[vmem] * (3 + len(images)) + [anywhere] * len(pieces),
            out_specs=[vmem] * len(outs),
            scratch_shapes=[pltpu.VMEM((n, pixels), BF16), dma((1,))],
            compiler_params=pltpu.CompilerParams(vmem_limit_bytes=12 << 20),
        )(lhs, cosines, sines, *images, *pieces)

    def evaluate(group, early=()):
        steps, tables, products = zip(*group)
        return pl.pallas_call(
            functools.partial(
                last_kernel, (n_img, len(early), steps, shifts, tiles, sig, n)
            ),
            name="last",
            out_shape=[jax.ShapeDtypeStruct((1, LANES), F32)] * n_img,
            in_specs=[vmem] * (2 * n_img - 1 + 2 * len(group) + len(early)),
            out_specs=[vmem] * n_img,
            compiler_params=pltpu.CompilerParams(
                vmem_limit_bytes=(12 << 20) if n_img < 4 else (40 << 20)
            ),
        )(*firsts, *rests, *tables, *products, *early)

    made = [((0, 0), *own)]
    for (low, high), near in zip(order, direct):
        mate = lax.ppermute(near, "dom", swap)
        made.append(((low, high), *make_table(near)))
        made.append(((high, low), *make_table(mate)))
    far_half = lax.ppermute(near_half, "dom", swap)
    late_table, late_product, late_cross = make_table(
        near_half, far_half, images=firsts
    )
    made.append(((last, last), late_table, late_product))
    found = []
    while len(made) > SET:
        found.append(evaluate(made[:SET]))
        made = made[SET:]
    ready = [table for _, table, _ in made[:-1]]
    early = pl.pallas_call(
        functools.partial(first_kernel, len(ready), shifts * n),
        name="first",
        out_shape=jax.ShapeDtypeStruct(
            (len(ready) * shifts * n, (n_img - 1) * 2 * rows), F32
        ),
        in_specs=[vmem] * (len(ready) + n_img - 1),
        out_specs=vmem,
        compiler_params=pltpu.CompilerParams(
            vmem_limit_bytes=(12 << 20) if n_img < 4 else (40 << 20)
        ),
    )(*ready, *firsts)
    found.append(evaluate(made, (early, late_cross)))
    evidence = found[0]
    for more in found[1:]:
        evidence = [a + b for a, b in zip(evidence, more)]
    gathered = [evidence[0]] + [across(evidence[k], k) for k in range(1, n_cls)]
    post, log_total = pl.pallas_call(
        functools.partial(finish_kernel, rows),
        name="finish",
        out_shape=[
            jax.ShapeDtypeStruct((n_cls, rows), F32),
            jax.ShapeDtypeStruct((1, rows), F32),
        ],
        in_specs=[vmem] * n_cls,
        out_specs=[vmem, vmem],
        compiler_params=pltpu.CompilerParams(vmem_limit_bytes=8 << 20),
    )(*gathered)
    return (post.T, log_total.reshape(rows))


def solution(mesh):
    placed = (
        P(("groups", "orient", "cls", "dom"), None, None),
        P(("groups", "orient", "cls", "dom")),
        P(("groups", "orient", "cls", "dom")),
        P(("groups", "orient", "cls", "dom"), None),
        P(),
        P(("groups", "cls"), "orient", None, None, None),
        P("groups", None),
    )

    return jax.shard_map(
        local,
        mesh=mesh,
        in_specs=placed,
        out_specs=(
            P(("groups", "orient", "cls", "dom"), None),
            P(("groups", "orient", "cls", "dom")),
        ),
        check_vma=False,
    )
```

```python
import functools
import math

import jax
import jax.numpy as jnp
from jax import lax
from jax.experimental import pallas as pl
from jax.experimental.pallas import tpu as pltpu
from jax.sharding import PartitionSpec as P


BOX = 256
KX = 129
KY = 128

EPSILON = 1e-06
LANES = 128
UNROLL = 43
SET = 4
F32 = jnp.float32
BF16 = jnp.bfloat16
CONTRACT_LAST = (((1,), (1,)), ((), ()))


def lane(k, width=1, count=None):
    return pl.ds(pl.multiple_of(k * width * LANES, LANES), (count or width) * LANES)


def iota(shape, axis):
    return lax.broadcasted_iota(jnp.int32, shape, axis)


def weighted(pick, ctf, raw, span):
    value = raw[:, span].astype(F32)
    chosen = jnp.dot(pick, ctf[:, span], preferred_element_type=F32)
    return (chosen * value).astype(BF16), jnp.sum(value * value, axis=1, keepdims=True)


def picked(code, n_codes):
    shape = (code.shape[0], n_codes)
    return (code[:, 0:1] == iota(shape, 1)).astype(BF16)


def weigh_kernel(dims, codes_in, beta_in, groups_in, offsets_in, particles, ctf_in, refs,
                 first, raw, ctf, more, part, turns,
                 codes, beta, groups, offsets, sem, ctf_sem, half_sem, small_sem):
    rows, per_block, n_codes, sig = dims
    half = part.shape[0]
    small = [
        pltpu.make_async_copy(codes_in, codes, small_sem.at[0]),
        pltpu.make_async_copy(groups_in, groups, small_sem.at[1]),
        pltpu.make_async_copy(beta_in, beta, small_sem.at[2]),
        pltpu.make_async_copy(offsets_in, offsets, small_sem.at[3]),
    ]
    for copy in small:
        copy.start()
    cut, pixels = first.shape[1], raw.shape[1]
    spans = (slice(0, cut), slice(cut, pixels))
    loads = []
    for b, span in enumerate(spans):
        copies = [pltpu.make_async_copy(ctf_in.at[:, span], ctf.at[:, span], ctf_sem.at[b])]
        for p in range(rows):
            copies.append(
                pltpu.make_async_copy(
                    particles.at[p, :, span], raw.at[2 * p : 2 * p + 2, span], sem.at[b]
                )
            )
        loads.append(copies)
        for copy in copies:
            copy.start()
    half_copy = pltpu.make_async_copy(
        refs.at[pl.ds(lax.axis_index("dom") * half, half)], part, half_sem
    )
    half_copy.start()
    shape = (2 * rows, LANES)
    owner = iota(shape, 0) // 2
    column = iota(shape, 1)
    for copy in small:
        copy.wait()
    noise = beta[...].astype(F32)
    noise = jnp.where(iota((2 * rows, rows), 0) // 2 == iota((2 * rows, rows), 1), noise, 0.0)
    extra = jnp.where(column == 1, jnp.sum(noise, axis=1, keepdims=True), 0.0)
    code = jnp.zeros(shape, jnp.int32)
    for p in range(rows):
        mine = owner == p
        code = jnp.where(mine, codes[p], code)
        for s in range(sig):
            group = groups[s, p // per_block].astype(F32)
            extra = jnp.where(mine & (column == 2 + s), group, extra)
    extra = jnp.where(column == 0, code.astype(F32), extra)
    pick = picked(code, n_codes)
    for copy in loads[0]:
        copy.wait()
    first[...], power = weighted(pick, ctf, raw, spans[0])
    more[...] = jnp.where(column == 2 + sig, power, extra)
    shape = turns.shape[1:]
    step_x = jnp.zeros(shape, jnp.int32)
    step_y = jnp.zeros(shape, jnp.int32)
    for t in range(offsets.shape[1]):
        step_x = jnp.where(iota(shape, 0) == t, offsets[0, t], step_x)
        step_y = jnp.where(iota(shape, 0) == t, offsets[1, t], step_y)
    turns[0] = step_x * iota(shape, 1) - step_y * (KY // 2)
    turns[1] = step_y - step_x
    turns[2] = step_x * KX - step_y
    half_copy.wait()
    for copy in loads[1]:
        copy.wait()


def rest_kernel(sig, raw, ctf, more, rest):
    pixels, cut = raw.shape[1], raw.shape[1] + LANES - rest.shape[1]
    extra = more[...]
    column = iota(extra.shape, 1)
    pick = picked(extra.astype(jnp.int32), ctf.shape[0])
    rest[:, : pixels - cut], power = weighted(pick, ctf, raw, slice(cut, pixels))
    power = power + extra[:, 2 + sig : 3 + sig]
    for s in range(3):
        term = power.astype(BF16).astype(F32)
        extra = jnp.where(column == 2 + sig + s, term, extra)
        power = power - term
    rest[:, pixels - cut :] = extra.astype(BF16)


def up(value, to):
    return -(-value // to) * to


def block_copies(sources, raw, sem, b, width):
    span = lane(b * width, 1, width)
    copies, row = [], 0
    for source in sources:
        for i in range(source.shape[0]):
            copies.append(
                pltpu.make_async_copy(
                    source.at[i, :, span], raw.at[row : row + 2, span], sem.at[b]
                )
            )
            row += 2
    return copies


def load_blocks(sources, raw, sem):
    count = sem.shape[0]
    for b in range(count):
        for copy in block_copies(sources, raw, sem, b, raw.shape[1] // LANES // count):
            copy.start()


def build_table(sources, raw, sem, cosines, sines, lhs, table, product, shifts, images=(), cross=None):
    n = raw.shape[0]
    odd = iota((n, LANES), 0) % 2 == 1
    count = sem.shape[0]
    width = raw.shape[1] // LANES // count

    def block(b, carry):
        for copy in block_copies(sources, raw, sem, b, width):
            copy.wait()

        def step(k, carry):
            here = lane(b * width + k)
            value = raw[:, here].astype(F32)
            turned = jnp.where(odd, -pltpu.roll(value, 1, 0), pltpu.roll(value, n - 1, 0))
            parts = [
                value * cosines[t : t + 1, here] + turned * sines[t : t + 1, here]
                for t in range(shifts)
            ]
            square = value * value
            high = square.astype(BF16).astype(F32)
            parts += [high, square - high]
            for i in range(0, len(parts), 2):
                both = jnp.concatenate(parts[i : i + 2], axis=0)
                table[n * i : n * i + both.shape[0], here] = both.astype(BF16)
            return carry

        return lax.fori_loop(0, width, step, carry, unroll=min(UNROLL, width))

    lax.fori_loop(0, count, block, 0)
    if not images:
        product[...] = lax.dot_general(
            table[...], lhs[...], CONTRACT_LAST, preferred_element_type=F32
        )
        return
    cut, width = images[0].shape[1], lhs.shape[0]
    right = jnp.concatenate([lhs[:, :cut]] + [image[...] for image in images], axis=0)
    both = lax.dot_general(
        table[:, :cut], right, CONTRACT_LAST, preferred_element_type=F32
    )
    product[...] = both[:, :width] + lax.dot_general(
        table[:, cut:], lhs[:, cut:], CONTRACT_LAST, preferred_element_type=F32
    )
    cross[...] = both[: cross.shape[0], width:]


def prepare_kernel(shifts, first, rest, ctf, turns, refs, lhs, cosines, sines, table, product, raw, sem):
    load_blocks([refs], raw, sem)
    rows, codes = first.shape[0], ctf.shape[0]
    cut = first.shape[1]
    lhs[:rows, :cut] = first[...]
    lhs[:rows, cut:] = rest[:, : lhs.shape[1] - cut]
    place = iota(turns.shape[1:], 1)
    base, slope, wrapped = turns[0], turns[1], turns[2]

    def step(k, carry):
        value = ctf[:, lane(k)].astype(F32)
        square = value * value
        high = square.astype(BF16)
        lhs[rows : rows + codes, lane(k)] = high
        lhs[rows + codes :, lane(k)] = (square - high.astype(F32)).astype(BF16)
        turn = (base + slope * k + jnp.where(place < k, wrapped, 0)) & (BOX - 1)
        quarter = (turn + BOX // 8) >> 6
        x = (turn - (quarter << 6)).astype(F32) * (2.0 * math.pi / BOX)
        x2 = x * x
        sin = x + x * x2 * (
            -1.6666654611e-1 + x2 * (8.3321608736e-3 + x2 * -1.9515295891e-4)
        )
        cos = (1.0 - 0.5 * x2) + x2 * x2 * (
            4.166664568298827e-2 + x2 * (-1.388731625493765e-3 + x2 * 2.443315711809948e-5)
        )
        swap = (quarter & 1) == 1
        near = jnp.where(swap, sin, cos)
        other = jnp.where(swap, cos, sin)
        cosines[:, lane(k)] = jnp.where(((quarter + 1) & 2) == 2, -near, near)
        sines[:, lane(k)] = jnp.where((quarter & 2) == 2, -other, other)
        return carry

    lax.fori_loop(0, lhs.shape[1] // LANES, step, 0, unroll=UNROLL)
    build_table([refs], raw, sem, cosines, sines, lhs, table, product, shifts)


def tables_kernel(shifts, n_other, lhs, cosines, sines, *refs):
    images, refs = refs[:n_other], refs[n_other:]
    raw, sem = refs[-2:]
    n_out = 3 if images else 2
    pieces, outs = refs[: -2 - n_out], refs[-2 - n_out : -2]
    load_blocks(pieces, raw, sem)
    build_table(pieces, raw, sem, cosines, sines, lhs, outs[0], outs[1], shifts, images, outs[-1])


def against(tables, used, span, images):
    stacked = jnp.concatenate([table[:used, span] for table in tables], axis=0)
    found = [
        lax.dot_general(
            stacked, image[:, : span.stop - span.start], CONTRACT_LAST, preferred_element_type=F32
        )
        for image in images
    ]
    return jnp.concatenate(found, axis=1) if len(found) > 1 else found[0]


def first_kernel(count, used, *refs):
    *inputs, out = refs
    tables, images = inputs[:count], inputs[count:]
    out[...] = against(tables, used, slice(0, images[0].shape[1]), images)


def last_kernel(dims, *refs):
    n_img, n_early, steps, shifts, tiles, sig, n = dims
    count = len(steps)
    refs = list(refs)
    z, d = lax.axis_index("orient"), lax.axis_index("dom")
    firsts = [refs.pop(0) for _ in range(n_img - 1)]
    rests = [refs.pop(0) for _ in range(n_img)]
    tables = [refs.pop(0) for _ in range(count)]
    products = [refs.pop(0) for _ in range(count)]
    starts = [refs.pop(0)[...] for _ in range(n_early)]
    outs = refs
    pixels = tiles * LANES
    rows = rests[0].shape[0]
    codes = (products[0].shape[1] - rows) // 2
    total_rows = n_img * rows
    used = shifts * n
    beyond = rests[0].shape[1] - LANES

    crossed = against(tables, used, slice(pixels - beyond, pixels), rests[1:])
    if not starts:
        starts = [against(tables, used, slice(0, pixels - beyond), firsts)]
    crossed = crossed + (jnp.concatenate(starts, axis=0) if len(starts) > 1 else starts[0])
    extra = jnp.concatenate([rest[:, beyond:] for rest in rests], axis=0)
    take = (iota((16, LANES), 0) == iota((16, LANES), 1)).astype(BF16)
    turned = lax.dot_general(take, extra, CONTRACT_LAST, preferred_element_type=F32)
    beta = turned[1:2]
    power = turned[2 + sig : 3 + sig] + turned[3 + sig : 4 + sig] + turned[4 + sig : 5 + sig]
    power = power + pltpu.roll(power, total_rows - 1, 1)
    column = iota((total_rows, 6 * codes), 1)
    pick = (extra[:, 0:1].astype(F32).astype(jnp.int32) == column % codes).astype(BF16)
    squares = jnp.concatenate(
        [product[shifts * n : (shifts + 2) * n, rows:] for product in products], axis=0
    )
    terms = []
    for _ in range(3):
        term = squares.astype(BF16)
        terms.append(term)
        squares = squares - term.astype(F32)
    energies = lax.dot_general(
        jnp.concatenate(terms, axis=1), pick, CONTRACT_LAST, preferred_element_type=F32
    )

    even_row = iota((n, total_rows), 0) % 2 == 0
    same = (iota((n, total_rows), 0) % 2) == (iota((n, total_rows), 1) % 2)
    evidence = jnp.zeros((n, total_rows), F32)
    for c in range(count):
        energy = energies[2 * c * n : (2 * c + 1) * n] + energies[(2 * c + 1) * n : (2 * c + 2) * n]
        energy = energy + pltpu.roll(energy, n - 1, 0)
        scale = beta * lax.rsqrt(power * energy + EPSILON)
        cross = jnp.concatenate(
            [products[c][:used, :rows], crossed[c * used : (c + 1) * used]], axis=1
        )
        total = jnp.zeros((n, total_rows), F32)
        for t in range(shifts):
            value = jnp.where(same, cross[t * n : (t + 1) * n], 0.0)
            value = value + pltpu.roll(value, n - 1, 0)
            value = value + pltpu.roll(value, total_rows - 1, 1)
            total = total + jnp.exp(jnp.where(same & even_row, value * scale, 0.0))
        gid = (z ^ jnp.where(d == 0, *steps[c])).astype(F32)
        named = turned[2:3] == gid
        for s in range(1, sig):
            named = named | (turned[2 + s : 3 + s] == gid)
        evidence = evidence + jnp.where(even_row & named, total, 0.0)
    evidence = jnp.sum(evidence, axis=0, keepdims=True)
    spread = jnp.concatenate(
        [evidence, jnp.zeros((1, LANES - total_rows % LANES), F32)], axis=1
    ) if total_rows % LANES else evidence
    for i in range(n_img):
        here = spread if i == 0 else pltpu.roll(spread, LANES - i * rows, 1)
        outs[i][...] = jnp.where(iota((1, LANES), 1) < rows, here, 1.0)


def finish_kernel(rows, *refs):
    n_cls = len(refs) - 2
    post, log_out = refs[-2:]
    x = lax.axis_index("cls")
    place = iota((1, LANES), 1)
    used = (place % 2 == 0) & (place < 2 * rows)
    found = [jnp.where(used, r[...], 1.0) for r in refs[:n_cls]]
    total = found[0]
    for value in found[1:]:
        total = total + value
    row = iota((n_cls, LANES), 0)
    table = jnp.zeros((n_cls, LANES), F32)
    for k in range(n_cls):
        table = jnp.where(row == (x ^ k), found[k], table)
    squeeze = (iota((LANES, rows), 0) == 2 * iota((LANES, rows), 1)).astype(F32)
    both = jnp.concatenate([table / total, jnp.log(total)], axis=0)
    both = jnp.dot(both, squeeze, precision=lax.Precision.HIGHEST, preferred_element_type=F32)
    post[...] = both[:n_cls]
    log_out[...] = both[n_cls:]


def local(particles, ctf_index, beta, significant, ctf_table, references, offsets):
    groups = lax.axis_size("orient")
    n_cls = lax.axis_size("cls")
    cores = lax.axis_size("dom")
    blocks_here, sig = significant.shape
    rows, _, pixels = particles.shape
    per_block = rows // blocks_here
    codes = ctf_table.shape[0]
    oris = references.shape[2]
    shifts = offsets.shape[0]
    tiles = pixels // LANES
    refs_own = references.reshape(oris, 2, pixels)
    steps = [k for k in range(1, groups) if k != groups // 2] + [groups // 2]
    anywhere = pl.BlockSpec(memory_space=pl.ANY)
    vmem = pl.BlockSpec(memory_space=pltpu.VMEM)
    hbm = pl.BlockSpec(memory_space=pltpu.HBM)
    dma = pltpu.SemaphoreType.DMA

    def in_hbm(values):
        return pltpu.with_memory_space_constraint(values, pltpu.HBM)

    def core_step(first, second):
        pairs = []
        for a in range(groups):
            for core in range(cores):
                step = second if core else first
                pairs.append((a * cores + core, (a ^ step) * cores + core))
        return pairs

    swap = [(c, cores - 1 - c) for c in range(cores)]
    direct, order = [], []
    while len(steps) > 1:
        low, high = steps.pop(0), steps.pop(0)
        direct.append(lax.ppermute(refs_own, ("orient", "dom"), core_step(low, high)))
        order.append((low, high))
    last = steps.pop(0)

    def across(values, k):
        return lax.ppermute(values, "cls", [(c, c ^ k) for c in range(n_cls)])

    half = oris // 2
    cut = tiles * 3 // 4 * LANES
    first, raw_rows, ctf_near, more, part, turns = pl.pallas_call(
        functools.partial(weigh_kernel, (rows, per_block, codes, sig)),
        name="weigh",
        out_shape=[
            jax.ShapeDtypeStruct((2 * rows, cut), BF16),
            jax.ShapeDtypeStruct((2 * rows, pixels), BF16),
            jax.ShapeDtypeStruct((codes, pixels), BF16),
            jax.ShapeDtypeStruct((2 * rows, LANES), F32),
            jax.ShapeDtypeStruct((half, 2, pixels), BF16),
            jax.ShapeDtypeStruct((3, up(shifts, 8), LANES), jnp.int32),
        ],
        in_specs=[hbm] * 7,
        out_specs=[vmem] * 6,
        scratch_shapes=[
            pltpu.SMEM((rows,), jnp.int32),
            pltpu.VMEM((1, rows), BF16),
            pltpu.SMEM((sig, blocks_here), jnp.int32),
            pltpu.SMEM((2, shifts), jnp.int32),
            dma((2,)),
            dma((2,)),
            dma,
            dma((4,)),
        ],
        compiler_params=pltpu.CompilerParams(vmem_limit_bytes=16 << 20),
    )(
        in_hbm(ctf_index),
        in_hbm(beta[None]),
        in_hbm(significant.T),
        in_hbm(offsets.T),
        in_hbm(particles),
        in_hbm(ctf_table),
        in_hbm(refs_own),
    )
    rest = pl.pallas_call(
        functools.partial(rest_kernel, sig),
        name="rest",
        out_shape=jax.ShapeDtypeStruct((2 * rows, pixels - cut + LANES), BF16),
        in_specs=[vmem] * 3,
        out_specs=vmem,
        compiler_params=pltpu.CompilerParams(vmem_limit_bytes=12 << 20),
    )(raw_rows, ctf_near, more)
    firsts, rests = [], [rest]
    for k in range(1, n_cls):
        firsts.append(across(first, k))
        rests.append(across(rest, k))
    near_half = lax.ppermute(part, "orient", [(a, a ^ last) for a in range(groups)])
    lhs_rows = 2 * rows + 2 * codes
    phase_shape = jax.ShapeDtypeStruct((up(shifts, 8), pixels), F32)
    n = 2 * oris
    n_img = n_cls
    n_blocks = 3 if tiles % 3 == 0 else 1

    used = (shifts + 2) * n
    lhs, cosines, sines, *own = pl.pallas_call(
        functools.partial(prepare_kernel, shifts),
        name="prepare",
        out_shape=[
            jax.ShapeDtypeStruct((lhs_rows, pixels), BF16),
            phase_shape,
            phase_shape,
            jax.ShapeDtypeStruct((used, pixels), BF16),
            jax.ShapeDtypeStruct((used, lhs_rows), F32),
        ],
        in_specs=[vmem] * 4 + [hbm],
        out_specs=[vmem] * 5,
        scratch_shapes=[pltpu.VMEM((n, pixels), BF16), dma((n_blocks,))],
        compiler_params=pltpu.CompilerParams(vmem_limit_bytes=16 << 20),
    )(first, rest, ctf_near, turns, in_hbm(refs_own))

    def make_table(*pieces, images=()):
        outs = [
            jax.ShapeDtypeStruct((used, pixels), BF16),
            jax.ShapeDtypeStruct((used, lhs_rows), F32),
        ]
        if images:
            outs.append(
                jax.ShapeDtypeStruct((shifts * n, len(images) * 2 * rows), F32)
            )
        return pl.pallas_call(
            functools.partial(tables_kernel, shifts, len(images)),
            name="tables",
            out_shape=outs,
            in_specs=[vmem] * (3 + len(images)) + [anywhere] * len(pieces),
            out_specs=[vmem] * len(outs),
            scratch_shapes=[pltpu.VMEM((n, pixels), BF16), dma((n_blocks,))],
            compiler_params=pltpu.CompilerParams(vmem_limit_bytes=12 << 20),
        )(lhs, cosines, sines, *images, *pieces)

    def evaluate(group, early=()):
        steps, tables, products = zip(*group)
        return pl.pallas_call(
            functools.partial(
                last_kernel, (n_img, len(early), steps, shifts, tiles, sig, n)
            ),
            name="last",
            out_shape=[jax.ShapeDtypeStruct((1, LANES), F32)] * n_img,
            in_specs=[vmem] * (2 * n_img - 1 + 2 * len(group) + len(early)),
            out_specs=[vmem] * n_img,
            compiler_params=pltpu.CompilerParams(
                vmem_limit_bytes=(12 << 20) if n_img < 4 else (40 << 20)
            ),
        )(*firsts, *rests, *tables, *products, *early)

    made = [((0, 0), *own)]
    for (low, high), near in zip(order, direct):
        mate = lax.ppermute(near, "dom", swap)
        made.append(((low, high), *make_table(near)))
        made.append(((high, low), *make_table(mate)))
    far_half = lax.ppermute(near_half, "dom", swap)
    late_table, late_product, late_cross = make_table(
        near_half, far_half, images=firsts
    )
    made.append(((last, last), late_table, late_product))
    found = []
    while len(made) > SET:
        found.append(evaluate(made[:SET]))
        made = made[SET:]
    ready = [table for _, table, _ in made[:-1]]
    early = pl.pallas_call(
        functools.partial(first_kernel, len(ready), shifts * n),
        name="first",
        out_shape=jax.ShapeDtypeStruct(
            (len(ready) * shifts * n, (n_img - 1) * 2 * rows), F32
        ),
        in_specs=[vmem] * (len(ready) + n_img - 1),
        out_specs=vmem,
        compiler_params=pltpu.CompilerParams(
            vmem_limit_bytes=(12 << 20) if n_img < 4 else (40 << 20)
        ),
    )(*ready, *firsts)
    found.append(evaluate(made, (early, late_cross)))
    evidence = found[0]
    for more in found[1:]:
        evidence = [a + b for a, b in zip(evidence, more)]
    gathered = [evidence[0]] + [across(evidence[k], k) for k in range(1, n_cls)]
    post, log_total = pl.pallas_call(
        functools.partial(finish_kernel, rows),
        name="finish",
        out_shape=[
            jax.ShapeDtypeStruct((n_cls, rows), F32),
            jax.ShapeDtypeStruct((1, rows), F32),
        ],
        in_specs=[vmem] * n_cls,
        out_specs=[vmem, vmem],
        compiler_params=pltpu.CompilerParams(vmem_limit_bytes=8 << 20),
    )(*gathered)
    return (post.T, log_total.reshape(rows))


def solution(mesh):
    placed = (
        P(("groups", "orient", "cls", "dom"), None, None),
        P(("groups", "orient", "cls", "dom")),
        P(("groups", "orient", "cls", "dom")),
        P(("groups", "orient", "cls", "dom"), None),
        P(),
        P(("groups", "cls"), "orient", None, None, None),
        P("groups", None),
    )

    return jax.shard_map(
        local,
        mesh=mesh,
        in_specs=placed,
        out_specs=(
            P(("groups", "orient", "cls", "dom"), None),
            P(("groups", "orient", "cls", "dom")),
        ),
        check_vma=False,
    )
```
